256 devices in a mesh: dp: 16 (over y, z_hi), ctx: 16 (over x, z_lo, core).
Axes of the slice: x: 4, y: 4, z: 8 (z_hi: 4, z_lo: 2; z = z_hi * 2 + z_lo), core: 2. Of those that a mesh axis runs over, the one named last changes fastest.
Arguments:
- frames: bfloat16 [16, 2048, 1024], P('dp', 'ctx'), may hold values from -6.5 to 6.5
- utt_lengths: int32 [16, 8], P('dp'), may hold values from 1 to 1152, 2048 in all within a row
- cotangent: bfloat16 [16, 2048, 1024], P('dp', 'ctx'), may hold values from -6 to 6
- w_dw: float32 [31, 1024], replicated, may hold values from -1 to 1
- w_kv: bfloat16 [1024, 2048], replicated
Outputs:
- output: bfloat16 [16, 2048, 1024], P('dp', 'ctx')
- dframes: bfloat16 [16, 2048, 1024], P('dp', 'ctx')
- grad_kv: float32 [1024, 2048], P(('dp', 'ctx'))
- grad_dw: float32 [1024, 31], P(('dp', 'ctx'))
The draws below stay inside these ranges and needn't reach their ends.
Inputs may be any that keep to these rules, and one draw needn't show every extreme that they name: `utt_lengths`: each row lists the frame counts of the utterances packed one after another into that sequence; they sum to 2048 and the longest is exactly 1152.
All inputs are finite; a program needn't handle non-finite values.
Results may differ from the reference program's by a relative error of at most 0.018.
Values may be sent and summed in bfloat16 or wider, within the bound.
A program may use at most 128 MiB of HBM per device.

```python
import math
import jax
import jax.numpy as jnp
import numpy as np
from jax import lax

D = 1024
H = 16
HD = 64
KERNEL = 31
TOK_DEV = 128
SEQ_LEN = 2048
SEQS = 16
UTTS = 8
MOST = 1152
N_CTX = 16


def draw_frames(key, part):
    base_key = jax.random.fold_in(key, 11)
    return jnp.clip(jax.random.normal(base_key, (SEQS, SEQ_LEN, D), jnp.float32), -6.0, 6.0).astype(jnp.bfloat16)


def draw_w_kv(key, part):
    noise = jax.random.normal(jax.random.fold_in(key, 21), (D, 2 * D), jnp.float32) * (1.0 / D) ** 0.5
    return noise.astype(jnp.bfloat16)


def level_of(own_key, shape, split, least, top_value):
    def one(axis_at, shards_of):
        draws = jax.random.uniform(jax.random.fold_in(jax.random.fold_in(own_key, 6), axis_at), (shards_of,), jnp.float32, least / len(split), top_value / len(split))
        return jnp.repeat(jnp.exp(draws), shape[axis_at] // shards_of).reshape((-1,) + (1,) * (len(shape) - axis_at - 1))

    factor_of = one(*split[0])
    for cut in split[1:]:
        factor_of = factor_of * one(*cut)
    return factor_of


def split_up(number_of, total, bound, skew):
    weights = [(1 << 20) // math.isqrt(grade ** skew) + 1 for grade in range(2, number_of + 1)]
    surplus, counts = total - bound - (number_of - 1), [1] * (number_of - 1)
    while surplus > 0:
        free = [i for i in range(number_of - 1) if counts[i] < bound]
        pool, left = sum([weights[i] for i in free]), surplus
        for i in free:
            more = min(bound - counts[i], max(1, left * weights[i] // pool), surplus)
            counts[i] = counts[i] + more
            surplus = surplus - more
    return np.array([bound] + counts)


def ragged_sizes(rng, number_of, total, limit, lean):
    if number_of == 2:
        one = jax.random.randint(rng, (), max(1, total - limit), min(limit, total - 1) + 1)
        return jnp.stack([one, total - one])
    sizes = jnp.asarray(split_up(number_of, total, limit, lean), jnp.int32)
    couples = (number_of - 1) // 2
    giver, taker = sizes[1:1 + 2 * couples:2], sizes[2:2 + 2 * couples:2]
    room = jnp.minimum(giver - 1, limit - taker)
    moved = jax.random.randint(jax.random.fold_in(rng, 1), (couples,), 0, 1 << 20) % (room + 1)
    sizes = sizes.at[1:1 + 2 * couples:2].set(giver - moved).at[2:2 + 2 * couples:2].set(taker + moved)
    return sizes[jax.random.permutation(jax.random.fold_in(rng, 2), number_of)]


def bell_draw(own_key, dims, deviation, bound, shards=(), held_as=jnp.bfloat16):
    values = deviation * jax.random.normal(own_key, dims, jnp.float32)
    if shards:
        values = values * level_of(own_key, dims, shards, -0.22, 0.18)
    return jnp.clip(values, -bound, bound).astype(held_as)


def setup_inputs(seed: int = 0) -> dict:
    arg_keys = jax.random.split(jax.random.key(seed), 6)
    return {
        "frames": draw_frames(jax.random.fold_in(arg_keys[5], 71), 0),
        "utt_lengths": jax.vmap(lambda own: ragged_sizes(own, UTTS, SEQ_LEN, MOST, 2))(jax.random.split(arg_keys[1], SEQS)).reshape((SEQS, UTTS)).astype(jnp.int32),
        "cotangent": bell_draw(arg_keys[2], (SEQS, SEQ_LEN, D), 1.0, 6.0, ((0, 16), (1, 16))),
        "w_dw": bell_draw(arg_keys[3], (KERNEL, D), KERNEL ** -0.5, 1.0, (), jnp.float32),
        "w_kv": draw_w_kv(jax.random.fold_in(arg_keys[5], 71), 0),
    }


def segment_index(lengths, frame_pos, seq_total):
    utt_ends = jnp.cumsum(lengths).astype(jnp.int32)
    counted = lax.optimization_barrier(jnp.sum((utt_ends[None, :] <= frame_pos[:, None]).astype(jnp.int32), axis=1)).astype(jnp.int32)
    inside = (frame_pos >= 0) & (frame_pos < seq_total)
    return jnp.where(inside, counted, -1).astype(jnp.int32)

def tap_sum(source, wide_seg, own_seg, weight_rows, row_count):
    result = jnp.zeros((row_count, source.shape[1]), jnp.float32)
    for tap_pos in range(weight_rows.shape[0]):
        same_utt = wide_seg[tap_pos:tap_pos + row_count] == own_seg
        result = result + jnp.where(same_utt[:, None], source[tap_pos:tap_pos + row_count], 0.0) * weight_rows[tap_pos]
    return result

def tap_grads(source, wide_seg, own_seg, grad_rows, row_count, tap_count):
    columns = []
    for tap_pos in range(tap_count):
        same_utt = wide_seg[tap_pos:tap_pos + row_count] == own_seg
        columns.append(lax.optimization_barrier(jnp.sum(jnp.where(same_utt[:, None], source[tap_pos:tap_pos + row_count], 0.0) * grad_rows, axis=0)))
    return jnp.stack(columns, axis=1)

def silu_slope(pre_act):
    sigmoid_v = jax.nn.sigmoid(pre_act)
    return sigmoid_v * (1.0 + pre_act * (1.0 - sigmoid_v))

def reference(frames, utt_lengths, cotangent, w_dw, w_kv):
    rim_width = KERNEL // 2
    score_scale = 1.0 / math.sqrt(HD)
    frame_pos = jnp.arange(SEQ_LEN, dtype=jnp.int32)
    wide_pos = jnp.arange(SEQ_LEN + 2 * rim_width, dtype=jnp.int32) - rim_width

    def one_sequence(sums_in, inputs):
        grad_kv, grad_dw = sums_in
        seq_frames, lengths, seq_cot = inputs
        own_seg = segment_index(lengths, frame_pos, SEQ_LEN)
        wide_seg = segment_index(lengths, wide_pos, SEQ_LEN)
        padded = jnp.pad(seq_frames.astype(jnp.float32), ((rim_width, rim_width), (0, 0)))
        conv_out = tap_sum(padded, wide_seg, own_seg, w_dw, SEQ_LEN)
        hidden = (seq_frames.astype(jnp.float32) + jax.nn.silu(conv_out)).astype(jnp.bfloat16)
        kv_rows_all = jnp.dot(hidden, w_kv, preferred_element_type=jnp.float32).astype(jnp.bfloat16)
        key_heads = kv_rows_all[:, :D].reshape(SEQ_LEN, H, HD).astype(jnp.float32)
        value_heads = kv_rows_all[:, D:].reshape(SEQ_LEN, H, HD).astype(jnp.float32)
        query_blocks = hidden.reshape(N_CTX, TOK_DEV, H, HD).astype(jnp.float32)
        grad_blocks = seq_cot.reshape(N_CTX, TOK_DEV, H, HD).astype(jnp.float32)
        seg_blocks = own_seg.reshape(N_CTX, TOK_DEV)

        def one_block(block_in):
            query_blk, grad_blk, qseg_blk = block_in
            same_utt = (qseg_blk[:, None] == own_seg[None, :])[None]
            scores = jnp.einsum('thd,uhd->htu', query_blk, key_heads) * score_scale
            scores = jnp.where(same_utt, scores, -jnp.inf)
            row_top = lax.optimization_barrier(jnp.max(scores, axis=2, keepdims=True))
            exp_scores = jnp.where(same_utt, jnp.exp(scores - row_top), 0.0)
            attn_probs = exp_scores / lax.optimization_barrier(jnp.sum(exp_scores, axis=2, keepdims=True))
            probs_low = lax.optimization_barrier(attn_probs.astype(jnp.bfloat16)).astype(jnp.float32)
            attended = jnp.einsum('htu,uhd->thd', probs_low, value_heads)
            dprobs = jnp.einsum('thd,uhd->htu', grad_blk, value_heads)
            rowdot = jnp.transpose(lax.optimization_barrier(jnp.sum(grad_blk * attended, axis=2)))[:, :, None]
            dscores = lax.optimization_barrier((attn_probs * (dprobs - rowdot)).astype(jnp.bfloat16)).astype(jnp.float32)
            dquery = jnp.einsum('htu,uhd->thd', dscores, key_heads) * score_scale
            dkeys = jnp.einsum('htu,thd->uhd', dscores, query_blk) * score_scale
            dvalues = jnp.einsum('htu,thd->uhd', probs_low, grad_blk)
            block_part = jnp.concatenate([dkeys.reshape(SEQ_LEN, D), dvalues.reshape(SEQ_LEN, D)], axis=1).astype(jnp.bfloat16)
            return (attended.reshape(TOK_DEV, D), dquery.reshape(TOK_DEV, D), block_part)
        attended, dquery, block_parts = lax.map(one_block, (query_blocks, grad_blocks, seg_blocks))
        kv_grad = lax.optimization_barrier(jnp.sum(block_parts.astype(jnp.float32), axis=0)).astype(jnp.bfloat16)
        output = (hidden.astype(jnp.float32) + attended.reshape(SEQ_LEN, D)).astype(jnp.bfloat16)
        dhidden = seq_cot.astype(jnp.float32) + dquery.reshape(SEQ_LEN, D) + jnp.dot(kv_grad, w_kv.T, preferred_element_type=jnp.float32)
        dconv = (dhidden * silu_slope(conv_out)).astype(jnp.bfloat16)
        dconv_pad = jnp.pad(dconv.astype(jnp.float32), ((rim_width, rim_width), (0, 0)))
        dframes = (dhidden + tap_sum(dconv_pad, wide_seg, own_seg, w_dw[::-1], SEQ_LEN)).astype(jnp.bfloat16)
        grad_dw = grad_dw + tap_grads(padded, wide_seg, own_seg, dconv.astype(jnp.float32), SEQ_LEN, KERNEL)
        grad_kv = grad_kv + jnp.dot(hidden.T, kv_grad, preferred_element_type=jnp.float32)
        return ((grad_kv, grad_dw), (output, dframes))
    sums_start = (jnp.zeros((D, 2 * D), jnp.float32), jnp.zeros((D, KERNEL), jnp.float32))
    (grad_kv, grad_dw), (output, dframes) = lax.scan(one_sequence, sums_start, (frames, utt_lengths, cotangent))
    return (output, dframes, grad_kv, grad_dw)
```

```python
import functools
import math

import jax
import jax.numpy as jnp
from jax import lax
from jax.experimental import pallas as pl
from jax.experimental.pallas import tpu as pltpu
from jax.sharding import PartitionSpec as P

F32, BF16, I32 = jnp.float32, jnp.bfloat16, jnp.int32
MESH = pl.DeviceIdType.MESH
HD = 64
LANES = 128
TAPS = 31
RIM = 16
FAR = 1 << 20
QB = 2
CHUNK = 1024


def dot(a, b):
    return jnp.dot(a, b, preferred_element_type=F32)


def dot_last(a, b):
    return lax.dot_general(a, b, (((1,), (1,)), ((), ())), preferred_element_type=F32)


def lane_block(index, width=LANES):
    return pl.ds(pl.multiple_of(index * width, width), width)


def utt_bounds(len_ref, pos):
    end = jnp.int32(0)
    start_of = jnp.zeros(pos.shape, I32)
    end_of = jnp.full(pos.shape, FAR, I32)
    for u in range(len_ref.shape[1]):
        end = end + len_ref[0, u]
        start_of = jnp.where(end <= pos, end, start_of)
        end_of = jnp.minimum(end_of, jnp.where(end > pos, end, FAR))
    return start_of, end_of


def kernel(
    n,
    len_ref, fr_ref, cot_ref, wdw_ref, wkv_hbm,
    out_ref, dfr_ref, gkv_ref, gdw_ref,
    wkv, halo, halo2, pad, xs, ys, jlo, jhi, conv, hb, snd, rqv, hp, hall,
    qkt, vgt, r1, r2, sk, s_ref, acc, ad, kv, rad, rkv, kvt2,
    kvg, dh, dcb, g1s, g1r, pdw, w1s, w1r, s2, t2,
    local_sem, halo_send, halo_recv, halo2_send, halo2_recv, a_send, a_recv, h_send, h_recv,
    ad_send, ad_recv, kv_send, kv_recv, mate_send, mate_recv, g1_send, g1_recv,
    w1_send, w1_recv, t2_send, t2_recv,
):
    rows = fr_ref.shape[1]
    width = fr_ref.shape[2]
    blocks = width // LANES
    total = n * rows
    m = n
    me = lax.axis_index("ctx")
    seq = lax.axis_index("dp")
    core = lax.rem(me, 2)
    chip = lax.div(me, 2)
    mate = me + 1 - 2 * core
    scale = 1.0 / math.sqrt(HD)

    barrier = pltpu.get_barrier_semaphore()

    def greet_ctx(s, carry):
        pl.semaphore_signal(barrier, inc=1, device_id={"ctx": lax.rem(me + s, n)}, device_id_type=MESH)
        return carry

    def greet_dp(s, carry):
        other = lax.rem(seq + s, m)
        pl.semaphore_signal(barrier, inc=1, device_id={"dp": other}, device_id_type=MESH)
        pl.semaphore_signal(barrier, inc=1, device_id={"dp": other, "ctx": mate}, device_id_type=MESH)
        return carry

    lax.fori_loop(1, n, greet_ctx, 0)
    lax.fori_loop(1, m, greet_dp, 0)

    wkv_copy = pltpu.make_async_copy(wkv_hbm, wkv, local_sem)
    wkv_copy.start()

    low = lax.broadcasted_iota(I32, (rows, LANES), 1) < HD
    pos = me * rows + lax.broadcasted_iota(I32, (rows, LANES), 0)
    start_of, end_of = utt_bounds(len_ref, pos)
    jlo[...] = start_of - pos + TAPS // 2
    jhi[...] = end_of - pos + TAPS // 2
    sk[...] = utt_bounds(len_ref, lax.broadcasted_iota(I32, (8, total), 1))[0]
    r1[HD:LANES, :] = jnp.zeros((HD, total), BF16)
    r2[0:HD, :] = jnp.zeros((HD, total), BF16)
    acc[...] = jnp.zeros(acc.shape, F32)
    pdw[...] = jnp.zeros(pdw.shape, F32)

    def pad_own(b, carry):
        pad[b, RIM:RIM + rows] = fr_ref[0, :, lane_block(b)].astype(F32)
        return carry

    lax.fori_loop(0, blocks, pad_own, 0)

    pl.semaphore_wait(barrier, (n - 1) + 2 * (m - 1))

    right, left = lax.rem(me + 1, n), lax.rem(me + n - 1, n)

    def halo_copies(source, target, send, recv):
        return (
            pltpu.make_async_remote_copy(
                source.at[pl.ds(rows - RIM, RIM)], target.at[0], send.at[0], recv.at[0],
                device_id={"ctx": right}, device_id_type=MESH,
            ),
            pltpu.make_async_remote_copy(
                source.at[pl.ds(0, RIM)], target.at[1], send.at[1], recv.at[1],
                device_id={"ctx": left}, device_id_type=MESH,
            ),
        )

    def taps_in(j):
        if j < TAPS // 2:
            return j >= jlo[...]
        if j > TAPS // 2:
            return j < jhi[...]
        return None

    def masked(mask, value):
        return value if mask is None else jnp.where(mask, value, 0.0)

    halos = halo_copies(fr_ref.at[0], halo, halo_send, halo_recv)
    for copy in halos:
        copy.start()
    for copy in halos:
        copy.wait()

    def conv_block(b, carry):
        cols = lane_block(b)
        pad[b, 0:RIM] = halo[0, :, cols].astype(F32)
        pad[b, RIM + rows:2 * RIM + rows] = halo[1, :, cols].astype(F32)
        for r in range(8):
            xs[r, b] = pad[b, r + 1:r + 1 + rows + 24]
        result = jnp.zeros((rows, LANES), F32)
        for j in range(TAPS):
            a, r = divmod(j, 8)
            result = result + masked(taps_in(j), xs[r, b, 8 * a:8 * a + rows]) * wdw_ref[j:j + 1, cols]
        conv[b] = result
        hidden = pad[b, RIM:RIM + rows] + result / (1.0 + jnp.exp(-result))
        hb[:, cols] = hidden.astype(BF16)
        return carry

    lax.fori_loop(0, blocks, conv_block, 0)
    wkv_copy.wait()

    def roll_half(x):
        return pltpu.roll(x, HD, 1)

    def kv_block(b, carry):
        k_cols = dot(hb[...], wkv[:, lane_block(b, 256)])
        v_cols = dot(hb[...], wkv[:, lane_block(b + blocks // 2, 256)])
        qs = []
        for half in range(2):
            p = 2 * b + half
            q2 = hb[:, lane_block(p)].astype(F32)
            g2 = cot_ref[0, :, lane_block(p)].astype(F32)
            k2 = k_cols[:, half * LANES:(half + 1) * LANES]
            v2 = v_cols[:, half * LANES:(half + 1) * LANES]
            snd[2 * p, :, 0:LANES] = jnp.where(low, q2, roll_half(k2)).astype(BF16)
            snd[2 * p, :, LANES:] = jnp.where(low, v2, roll_half(g2)).astype(BF16)
            snd[2 * p + 1, :, 0:LANES] = jnp.where(low, roll_half(q2), k2).astype(BF16)
            snd[2 * p + 1, :, LANES:] = jnp.where(low, roll_half(v2), g2).astype(BF16)
            qs.append(q2)
        hp[0, :, lane_block(b)] = jnp.where(low, qs[0], roll_half(qs[1])).astype(BF16)
        hp[1, :, lane_block(b)] = jnp.where(low, roll_half(qs[0]), qs[1]).astype(BF16)
        return carry

    lax.fori_loop(0, blocks // 2, kv_block, 0)

    def exchange(source_of, target, send, recv):
        def copy_to(peer):
            return pltpu.make_async_remote_copy(
                source_of(peer), target.at[me], send.at[peer], recv.at[me],
                device_id={"ctx": peer}, device_id_type=MESH,
            )

        def copy_from(peer):
            return pltpu.make_async_remote_copy(
                source_of(peer), target.at[peer], send.at[peer], recv.at[peer],
                device_id={"ctx": peer}, device_id_type=MESH,
            )

        def start(s, carry):
            copy_to(lax.rem(me + s, n)).start()
            return carry

        def start_one(peer):
            @pl.when(peer != me)
            def _():
                copy_to(peer).start()

        def wait_recv(s, carry):
            copy_from(lax.rem(me + n - s, n)).wait_recv()
            return carry

        def wait_send(s, carry):
            copy_to(lax.rem(me + s, n)).wait_send()
            return carry

        return (
            lambda: lax.fori_loop(1, n, start, 0),
            start_one,
            lambda: lax.fori_loop(1, n, wait_recv, 0),
            lambda: lax.fori_loop(1, n, wait_send, 0),
        )

    a_start, _, a_wait, a_sent = exchange(lambda peer: snd.at[peer], rqv, a_send, a_recv)
    h_start, _, h_wait, h_sent = exchange(lambda peer: hp.at[lax.rem(peer, 2)], hall, h_send, h_recv)
    _, ad_start, ad_wait, ad_sent = exchange(lambda peer: ad.at[peer], rad, ad_send, ad_recv)
    kv_start, _, kv_wait, kv_sent = exchange(lambda peer: kv.at[peer], rkv, kv_send, kv_recv)
    t2_start, _, t2_wait, t2_sent = exchange(lambda peer: s2.at[peer], t2, t2_send, t2_recv)

    a_start()
    rqv[me] = snd[me]
    hall[me] = hp[core]
    a_wait()
    h_start()

    def turn(i, carry):
        cols = lane_block(i)
        qk_t = jnp.transpose(rqv[i, :, 0:LANES].astype(F32)).astype(BF16)
        vg_t = jnp.transpose(rqv[i, :, LANES:].astype(F32)).astype(BF16)
        qkt[:, cols] = qk_t
        vgt[:, cols] = vg_t
        r1[0:HD, cols] = qk_t[HD:LANES]
        r2[HD:LANES, cols] = vg_t[0:HD]
        return carry

    lax.fori_loop(0, n, turn, 0)

    q_rows = QB * rows
    q_low = lax.broadcasted_iota(I32, (q_rows, LANES), 1) < HD
    chunk_blocks = CHUNK // rows
    exp_scale = scale * math.log2(math.e)
    chunks = [slice(c * CHUNK, (c + 1) * CHUNK) for c in range(total // CHUNK)]

    def attend(i, carry):
        own = pl.ds(i * QB, QB)
        q = rqv[own, :, 0:LANES].reshape(q_rows, LANES)
        g = rqv[own, :, LANES:].reshape(q_rows, LANES)
        q_pos = i * q_rows + lax.broadcasted_iota(I32, (q_rows, 1), 0)
        sq = utt_bounds(len_ref, q_pos)[0]
        tops = []
        for cols in chunks:
            s = jnp.where(sq == sk[0:1, cols], dot(q, r1[:, cols]), -jnp.inf)
            s_ref[:, cols] = s
            tops.append(jnp.max(s, axis=1, keepdims=True))
        shift = functools.reduce(jnp.maximum, tops) * exp_scale
        sums = []
        for cols in chunks:
            e = jnp.exp2(s_ref[:, cols] * exp_scale - shift)
            s_ref[:, cols] = e
            sums.append(jnp.sum(e, axis=1, keepdims=True))
        inv = 1.0 / functools.reduce(jnp.add, sums)
        o = jnp.zeros((q_rows, LANES), F32)
        g_t = vgt[HD:LANES, lane_block(i, q_rows)]
        for c, cols in enumerate(chunks):
            probs = s_ref[:, cols] * inv
            s_ref[:, cols] = probs
            low_probs = probs.astype(BF16)
            these = slice(c * chunk_blocks, (c + 1) * chunk_blocks)
            o = o + dot(low_probs, rqv[these, :, LANES:].reshape(CHUNK, LANES))
            acc[HD:LANES, cols] += dot(g_t, low_probs)
        rowdot = jnp.sum(jnp.where(q_low, roll_half(g.astype(F32)) * o, 0.0), axis=1, keepdims=True)
        dq = jnp.zeros((q_rows, LANES), F32)
        q_t = qkt[0:HD, lane_block(i, q_rows)]
        for c, cols in enumerate(chunks):
            dscores = (s_ref[:, cols] * (dot(g, r2[:, cols]) - rowdot)).astype(BF16)
            these = slice(c * chunk_blocks, (c + 1) * chunk_blocks)
            dq = dq + dot(dscores, rqv[these, :, 0:LANES].reshape(CHUNK, LANES))
            acc[0:HD, cols] += dot(q_t, dscores)
        ad[own] = jnp.where(q_low, o, dq * scale).astype(BF16).reshape(QB, rows, LANES)
        for r in range(QB):
            ad_start(i * QB + r)
        return carry

    lax.fori_loop(0, n // QB, attend, 0)

    def turn_back(i, carry):
        cols = lane_block(i)
        both = jnp.concatenate([acc[0:HD, cols] * scale, acc[HD:LANES, cols]], axis=0)
        kvt2[core, :, cols] = both.astype(BF16)
        kv[i] = jnp.transpose(both).astype(BF16)
        return carry

    lax.fori_loop(0, n, turn_back, 0)
    kv_start()
    mate_copy = pltpu.make_async_remote_copy(
        kvt2.at[core], kvt2.at[core], mate_send, mate_recv, device_id={"ctx": mate}, device_id_type=MESH
    )
    mate_copy.start()
    mate_arrival = pltpu.make_async_remote_copy(
        kvt2.at[1 - core], kvt2.at[1 - core], mate_send, mate_recv, device_id={"ctx": mate}, device_id_type=MESH
    )
    rad[me] = ad[me]
    rkv[me] = kv[me]

    ad_wait()

    def attended_block(p, carry):
        cols = lane_block(p)
        even, odd = rad[2 * p].astype(F32), rad[2 * p + 1].astype(F32)
        attended = jnp.where(low, even, roll_half(odd))
        dquery = jnp.where(low, roll_half(even), odd)
        out_ref[0, :, cols] = (hb[:, cols].astype(F32) + attended).astype(BF16)
        dh[p] = cot_ref[0, :, cols].astype(F32) + dquery
        return carry

    lax.fori_loop(0, blocks, attended_block, 0)
    kv_wait()

    def grad_block(p, carry):
        even, odd = rkv[2 * p].astype(F32), rkv[2 * p + 1].astype(F32)
        kvg[:, lane_block(p)] = jnp.where(low, even, roll_half(odd)).astype(BF16)
        kvg[:, lane_block(p + blocks)] = jnp.where(low, roll_half(even), odd).astype(BF16)
        return carry

    lax.fori_loop(0, blocks, grad_block, 0)

    def dhidden_block(b, carry):
        back = dot_last(kvg[...], wkv[lane_block(b, 256), :])
        for half in range(2):
            p = 2 * b + half
            dhidden = dh[p] + back[:, half * LANES:(half + 1) * LANES]
            dh[p] = dhidden
            v = conv[p]
            s = 1.0 / (1.0 + jnp.exp(-v))
            dcb[:, lane_block(p)] = (dhidden * (s * (1.0 + v * (1.0 - s)))).astype(BF16)
        return carry

    lax.fori_loop(0, blocks // 2, dhidden_block, 0)

    halos2 = halo_copies(dcb, halo2, halo2_send, halo2_recv)
    for copy in halos2:
        copy.start()

    h_wait()
    mate_arrival.wait_recv()
    part = jnp.transpose(dot(kvt2[...].reshape(2 * LANES, total), hall[...].reshape(total, width // 2)))
    for q in range(m // 2):
        for e in range(2):
            g1s[2 * q + e] = part[q * HD:(q + 1) * HD, e * LANES:(e + 1) * LANES].astype(BF16)

    def g1_copy(index):
        q, e = lax.div(index, 2), lax.rem(index, 2)
        return pltpu.make_async_remote_copy(
            g1s.at[index], g1r.at[seq], g1_send.at[index], g1_recv.at[seq],
            device_id={"dp": 2 * q + core, "ctx": 2 * chip + e}, device_id_type=MESH,
        )

    stays = lax.rem(seq, 2) == core
    own_piece = 2 * lax.div(seq, 2) + core

    def g1_start(index, carry):
        @pl.when(jnp.logical_not(stays & (index == own_piece)))
        def _():
            g1_copy(index).start()
        return carry

    lax.fori_loop(0, m, g1_start, 0)

    @pl.when(stays)
    def _():
        g1r[seq] = g1s[own_piece]

    for copy in halos2:
        copy.wait()

    def dframes_block(b, carry):
        cols = lane_block(b)
        own = dcb[:, cols].astype(F32)
        pad[b, 0:RIM] = halo2[0, :, cols].astype(F32)
        pad[b, RIM:RIM + rows] = own
        pad[b, RIM + rows:2 * RIM + rows] = halo2[1, :, cols].astype(F32)
        for r in range(8):
            ys[r] = pad[b, r + 1:r + 1 + rows + 24]
        result = dh[b]
        for j in range(TAPS):
            a, r = divmod(j, 8)
            mask = taps_in(j)
            here = slice(8 * a, 8 * a + rows)
            back = TAPS - 1 - j
            result = result + masked(mask, ys[r, here]) * wdw_ref[back:back + 1, cols]
            pdw[j:j + 1, cols] = jnp.sum(masked(mask, xs[r, b, here]) * own, axis=0, keepdims=True)
        dfr_ref[0, :, cols] = result.astype(BF16)
        turned = jnp.transpose(pdw[:, cols])
        for half in range(2):
            packed = None
            for k in range(4):
                slab = turned[half * HD + 16 * k:half * HD + 16 * (k + 1)]
                slab = slab if k == 0 else pltpu.roll(slab, 32 * k, 1)
                packed = slab if packed is None else packed + slab
            w1s[2 * b + half] = packed
        return carry

    lax.fori_loop(0, blocks, dframes_block, 0)

    def w1_to(s):
        other = lax.rem(seq + s, m)
        return pltpu.make_async_remote_copy(
            w1s.at[other], w1r.at[seq], w1_send.at[other], w1_recv.at[seq],
            device_id={"dp": other}, device_id_type=MESH,
        )

    def w1_start(s, carry):
        w1_to(s).start()
        return carry

    lax.fori_loop(1, m, w1_start, 0)
    w1r[seq] = w1s[seq]


    def g1_wait(d, carry):
        from_self = (d == seq) & stays
        @pl.when(jnp.logical_not(from_self))
        def _():
            pltpu.make_async_remote_copy(
                g1s.at[0], g1r.at[d], g1_send.at[0], g1_recv.at[d],
                device_id={"ctx": mate}, device_id_type=MESH,
            ).wait_recv()
        return carry

    lax.fori_loop(0, m, g1_wait, 0)

    def w1_wait(s, carry):
        d = lax.rem(seq + s, m)
        pltpu.make_async_remote_copy(
            w1s.at[d], w1r.at[d], w1_send.at[d], w1_recv.at[d],
            device_id={"dp": d}, device_id_type=MESH,
        ).wait_recv()
        return carry

    lax.fori_loop(1, m, w1_wait, 0)
    kv_rows = functools.reduce(jnp.add, [g1r[d].astype(F32) for d in range(m)])
    dw_rows = functools.reduce(jnp.add, [w1r[d] for d in range(m)])
    for k in range(4):
        turned = dw_rows if k == 0 else pltpu.roll(dw_rows, LANES - 32 * k, 1)
        for r in range(4):
            c = 4 * k + r
            s2[c, 0:4] = kv_rows[4 * c:4 * c + 4]
            s2[c, 4:8] = turned[4 * r:4 * r + 4]
    t2_start()
    t2[me] = s2[me]
    t2_wait()
    low4 = lax.broadcasted_iota(I32, (4, LANES), 1) < HD
    for p in range(blocks):
        even, odd = t2[2 * p, 0:4], t2[2 * p + 1, 0:4]
        gkv_ref[:, p * LANES:(p + 1) * LANES] = jnp.where(low4, even, roll_half(odd))
        gkv_ref[:, width + p * LANES:width + (p + 1) * LANES] = jnp.where(low4, roll_half(even), odd)
    gdw_ref[...] = functools.reduce(jnp.add, [t2[h, 4:8] for h in range(n)])[:, 0:TAPS]

    a_sent()
    h_sent()
    ad_sent()
    kv_sent()
    mate_copy.wait_send()

    def g1_sent(index, carry):
        @pl.when(jnp.logical_not(stays & (index == own_piece)))
        def _():
            g1_copy(index).wait_send()
        return carry

    lax.fori_loop(0, m, g1_sent, 0)

    def w1_sent(s, carry):
        w1_to(s).wait_send()
        return carry

    lax.fori_loop(1, m, w1_sent, 0)
    t2_sent()


def on_device(frames, utt_lengths, cotangent, w_dw, w_kv):
    n = lax.axis_size("ctx")
    rows, width = frames.shape[1], frames.shape[2]
    blocks = width // LANES
    total = n * rows
    dma = pltpu.SemaphoreType.DMA
    vmem = pltpu.VMEM
    scratch = [
        vmem(w_kv.shape, BF16),
        vmem((2, RIM, width), BF16),
        vmem((2, RIM, width), BF16),
        vmem((blocks, rows + 2 * RIM, LANES), F32),
        vmem((8, blocks, rows + 24, LANES), F32),
        vmem((8, rows + 24, LANES), F32),
        vmem((rows, LANES), I32),
        vmem((rows, LANES), I32),
        vmem((blocks, rows, LANES), F32),
        vmem((rows, width), BF16),
        vmem((n, rows, 2 * LANES), BF16),
        vmem((n, rows, 2 * LANES), BF16),
        vmem((2, rows, width // 2), BF16),
        vmem((n, rows, width // 2), BF16),
        vmem((LANES, total), BF16),
        vmem((LANES, total), BF16),
        vmem((LANES, total), BF16),
        vmem((LANES, total), BF16),
        vmem((8, total), I32),
        vmem((QB * rows, total), F32),
        vmem((LANES, total), F32),
        vmem((n, rows, LANES), BF16),
        vmem((n, rows, LANES), BF16),
        vmem((n, rows, LANES), BF16),
        vmem((n, rows, LANES), BF16),
        vmem((2, LANES, total), BF16),
        vmem((rows, 2 * width), BF16),
        vmem((blocks, rows, LANES), F32),
        vmem((rows, width), BF16),
        vmem((n, HD, LANES), BF16),
        vmem((n, HD, LANES), BF16),
        vmem((LANES, width), F32),
        vmem((n, 16, LANES), F32),
        vmem((n, 16, LANES), F32),
        vmem((n, 8, LANES), F32),
        vmem((n, 8, LANES), F32),
        dma, dma((2,)), dma((2,)), dma((2,)), dma((2,)),
        dma((n,)), dma((n,)), dma((n,)), dma((n,)),
        dma((n,)), dma((n,)), dma((n,)), dma((n,)), dma, dma,
        dma((n,)), dma((n,)), dma((n,)), dma((n,)), dma((n,)), dma((n,)),
    ]
    whole = pl.BlockSpec(memory_space=vmem)
    return pl.pallas_call(
        functools.partial(kernel, n),
        out_shape=(
            jax.ShapeDtypeStruct(frames.shape, BF16),
            jax.ShapeDtypeStruct(frames.shape, BF16),
            jax.ShapeDtypeStruct((4, 2 * width), F32),
            jax.ShapeDtypeStruct((4, TAPS), F32),
        ),
        in_specs=[pl.BlockSpec(memory_space=pltpu.SMEM), whole, whole, whole, pl.BlockSpec(memory_space=pl.ANY)],
        out_specs=(whole, whole, whole, whole),
        scratch_shapes=scratch,
        compiler_params=pltpu.CompilerParams(
            collective_id=0, has_side_effects=True, vmem_limit_bytes=56 << 20
        ),
    )(utt_lengths, frames, cotangent, w_dw, w_kv)


def solution(mesh):
    placed = (P("dp", "ctx", None), P("dp", None), P("dp", "ctx", None), P(), P())
    return jax.shard_map(
        on_device,
        mesh=mesh,
        in_specs=placed,
        out_specs=(
            P("dp", "ctx", None),
            P("dp", "ctx", None),
            P(("dp", "ctx"), None),
            P(("dp", "ctx"), None),
        ),
        check_vma=False,
    )
```

```python
import functools
import math

import jax
import jax.numpy as jnp
from jax import lax
from jax.experimental import pallas as pl
from jax.experimental.pallas import tpu as pltpu
from jax.sharding import PartitionSpec as P

F32, BF16, I32 = jnp.float32, jnp.bfloat16, jnp.int32
MESH = pl.DeviceIdType.MESH
HD = 64
LANES = 128
TAPS = 31
RIM = 16
FAR = 1 << 20
QB = 2
CHUNK = 1024
LATE = 5


def dot(a, b):
    return jnp.dot(a, b, preferred_element_type=F32)


def dot_last(a, b):
    return lax.dot_general(a, b, (((1,), (1,)), ((), ())), preferred_element_type=F32)


def lane_block(index, width=LANES):
    return pl.ds(pl.multiple_of(index * width, width), width)


def utt_bounds(len_ref, pos):
    end = jnp.int32(0)
    start_of = jnp.zeros(pos.shape, I32)
    end_of = jnp.full(pos.shape, FAR, I32)
    for u in range(len_ref.shape[1]):
        end = end + len_ref[0, u]
        start_of = jnp.where(end <= pos, end, start_of)
        end_of = jnp.minimum(end_of, jnp.where(end > pos, end, FAR))
    return start_of, end_of


def kernel(
    n,
    len_ref, fr_hbm, cot_hbm, wdw_hbm, wkv_hbm,
    out_ref, dfr_ref, gkv_ref, gdw_ref,
    fr, cot, wdw, wkv, halo, halo2, pad, xs, ys, jlo, jhi, conv, hb,
    g_snd, g_rcv, q_snd, q_rcv, f_snd, f_rcv, hp, hall,
    qg, qgt, kvt, sk, s_ref, acc, ad, kv, rad, rkv, kvt2,
    kvg, dh, dcb, g1s, g1r, pdw, w1s, w1r, s2, t2,
    local_sems, halo_send, halo_recv, halo2_send, halo2_recv,
    g_send, g_recv, q_send, q_recv, f_send, f_recv, h_send, h_recv,
    ad_send, ad_recv, kv_send, kv_recv, mate_send, mate_recv, across_send, across_recv, g1_send, g1_recv,
    w1_send, w1_recv, t2_send, t2_recv,
):
    rows, width = fr.shape
    blocks = width // LANES
    total = n * rows
    m = n
    me = lax.axis_index("ctx")
    seq = lax.axis_index("dp")
    core = lax.rem(me, 2)
    chip = lax.div(me, 2)
    mate = me + 1 - 2 * core
    side = lax.rem(chip, 2)
    across = me + 2 - 4 * side
    ring_spot = lax.div(chip, 2)
    scale = 1.0 / math.sqrt(HD)

    barrier = pltpu.get_barrier_semaphore()

    def greet_ctx(s, carry):
        pl.semaphore_signal(barrier, inc=1, device_id={"ctx": lax.rem(me + s, n)}, device_id_type=MESH)
        return carry

    def greet_dp(s, carry):
        other = lax.rem(seq + s, m)
        pl.semaphore_signal(barrier, inc=1, device_id={"dp": other}, device_id_type=MESH)
        pl.semaphore_signal(barrier, inc=1, device_id={"dp": other, "ctx": across}, device_id_type=MESH)
        return carry

    fr_copy = pltpu.make_async_copy(fr_hbm.at[0], fr, local_sems.at[0])
    wdw_copy = pltpu.make_async_copy(wdw_hbm, wdw, local_sems.at[1])
    cot_copy = pltpu.make_async_copy(cot_hbm.at[0], cot, local_sems.at[2])
    wkv_copy = pltpu.make_async_copy(wkv_hbm, wkv, local_sems.at[3])
    lax.fori_loop(1, m, greet_dp, 0)
    lax.fori_loop(1, n, greet_ctx, 0)
    for copy in (fr_copy, wdw_copy, cot_copy, wkv_copy):
        copy.start()

    low = lax.broadcasted_iota(I32, (rows, LANES), 1) < HD
    low_half = lax.broadcasted_iota(I32, (rows // 2, LANES), 1) < HD
    pos = me * rows + lax.broadcasted_iota(I32, (rows, LANES), 0)
    start_of, end_of = utt_bounds(len_ref, pos)
    jlo[...] = start_of - pos + TAPS // 2
    jhi[...] = end_of - pos + TAPS // 2

    def taps_in(j, part):
        if j < TAPS // 2:
            return j >= jlo[part]
        if j > TAPS // 2:
            return j < jhi[part]
        return None

    def masked(mask, value):
        return value if mask is None else jnp.where(mask, value, 0.0)

    def conv_part(b, first, last):
        cols = lane_block(b)
        part = slice(first, last)
        result = jnp.zeros((last - first, LANES), F32)
        for j in range(TAPS):
            a, r = divmod(j, 8)
            source = xs[r, b, 8 * a + first:8 * a + last]
            result = result + masked(taps_in(j, part), source) * wdw[j:j + 1, cols]
        conv[b, part] = result
        hidden = pad[b, RIM + first:RIM + last] + result / (1.0 + jnp.exp(-result))
        hb[part, cols] = hidden.astype(BF16)

    def conv_inner(b, carry):
        pad[b, RIM:RIM + rows] = fr[:, lane_block(b)].astype(F32)
        for r in range(8):
            xs[r, b, RIM:rows + 8] = pad[b, r + 1 + RIM:r + 1 + rows + 8]
        conv_part(b, RIM, rows - RIM)
        return carry

    def roll_half(x):
        return pltpu.roll(x, HD, 1)

    def split_heads(pair, target, p):
        top, bottom = pair[0:rows // 2], pair[rows // 2:]
        target[2 * p] = jnp.where(low_half, top, roll_half(bottom)).astype(BF16)
        target[2 * p + 1] = jnp.where(low_half, roll_half(top), bottom).astype(BF16)

    def pack_cotangent(p, carry):
        split_heads(cot[:, lane_block(p)].astype(F32), g_snd, p)
        return carry

    fr_copy.wait()
    wdw_copy.wait()
    pad[:, 0:RIM] = jnp.zeros((blocks, RIM, LANES), F32)
    pad[:, RIM + rows:2 * RIM + rows] = jnp.zeros((blocks, RIM, LANES), F32)
    lax.fori_loop(0, blocks, conv_inner, 0)
    cot_copy.wait()
    lax.fori_loop(0, blocks, pack_cotangent, 0)
    sk[...] = utt_bounds(len_ref, lax.broadcasted_iota(I32, (8, total), 1))[0]
    acc[...] = jnp.zeros(acc.shape, F32)
    pdw[...] = jnp.zeros(pdw.shape, F32)

    pl.semaphore_wait(barrier, (n - 1) + 2 * (m - 1))

    right, left = lax.rem(me + 1, n), lax.rem(me + n - 1, n)

    def halo_copies(source, target, send, recv):
        return (
            pltpu.make_async_remote_copy(
                source.at[pl.ds(rows - RIM, RIM)], target.at[0], send.at[0], recv.at[0],
                device_id={"ctx": right}, device_id_type=MESH,
            ),
            pltpu.make_async_remote_copy(
                source.at[pl.ds(0, RIM)], target.at[1], send.at[1], recv.at[1],
                device_id={"ctx": left}, device_id_type=MESH,
            ),
        )

    def exchange(source_of, target, send, recv):
        def copy_to(peer):
            return pltpu.make_async_remote_copy(
                source_of(peer), target(peer).at[me], send.at[peer], recv.at[me],
                device_id={"ctx": peer}, device_id_type=MESH,
            )

        def copy_from(peer):
            return pltpu.make_async_remote_copy(
                source_of(peer), target(me).at[peer], send.at[peer], recv.at[peer],
                device_id={"ctx": peer}, device_id_type=MESH,
            )

        def start(s, carry):
            copy_to(lax.rem(me + s, n)).start()
            return carry

        def start_one(peer):
            @pl.when(peer != me)
            def _():
                copy_to(peer).start()

        def wait_recv(s, carry):
            copy_from(lax.rem(me + n - s, n)).wait_recv()
            return carry

        def wait_send(s, carry):
            copy_to(lax.rem(me + s, n)).wait_send()
            return carry

        return (
            lambda first=1, last=n: lax.fori_loop(first, last, start, 0),
            start_one,
            lambda: lax.fori_loop(1, n, wait_recv, 0),
            lambda: lax.fori_loop(1, n, wait_send, 0),
        )

    g_start, _, g_wait, g_sent = exchange(lambda peer: g_snd.at[peer], lambda owner: g_rcv, g_send, g_recv)
    q_start, _, q_wait, q_sent = exchange(lambda peer: q_snd.at[peer], lambda owner: q_rcv, q_send, q_recv)
    _, f_start, f_wait, f_sent = exchange(lambda peer: f_snd.at[peer], lambda owner: f_rcv, f_send, f_recv)
    h_start, _, h_wait, h_sent = exchange(lambda peer: hp.at[lax.rem(peer, 4)], lambda owner: hall.at[lax.rem(owner, 2)], h_send, h_recv)
    _, ad_start, ad_wait, ad_sent = exchange(lambda peer: ad.at[peer], lambda owner: rad, ad_send, ad_recv)
    _, kv_start, kv_wait, kv_sent = exchange(lambda peer: kv.at[peer], lambda owner: rkv, kv_send, kv_recv)
    t2_start, _, t2_wait, t2_sent = exchange(lambda peer: s2.at[peer], lambda owner: t2, t2_send, t2_recv)

    halos = halo_copies(fr, halo, halo_send, halo_recv)
    for copy in halos:
        copy.start()
    g_start()
    for copy in halos:
        copy.wait()

    def conv_outer(b, carry):
        cols = lane_block(b)
        pad[b, 0:RIM] = halo[0, :, cols].astype(F32)
        pad[b, RIM + rows:2 * RIM + rows] = halo[1, :, cols].astype(F32)
        for r in range(8):
            xs[r, b, 0:RIM] = pad[b, r + 1:r + 1 + RIM]
            xs[r, b, rows + 8:rows + 24] = pad[b, r + 9 + rows:r + 25 + rows]
        conv_part(b, 0, RIM)
        conv_part(b, rows - RIM, rows)
        return carry

    lax.fori_loop(0, blocks, conv_outer, 0)

    def pack_hidden(b, carry):
        first, second = [hb[:, lane_block(2 * b + k)].astype(F32) for k in range(2)]
        split_heads(first, q_snd, 2 * b)
        split_heads(second, q_snd, 2 * b + 1)
        part = lane_block(lax.rem(b, 2))
        hp[lax.div(b, 2), :, part] = jnp.where(low, first, roll_half(second)).astype(BF16)
        hp[2 + lax.div(b, 2), :, part] = jnp.where(low, roll_half(first), second).astype(BF16)
        return carry

    lax.fori_loop(0, blocks // 2, pack_hidden, 0)
    q_start()
    wkv_copy.wait()

    def kv_block(b, carry):
        k_cols = dot(hb[...], wkv[:, lane_block(b, 256)])
        v_cols = dot(hb[...], wkv[:, lane_block(b + blocks // 2, 256)])
        for half in range(2):
            h = 2 * (2 * b + half)
            k2 = k_cols[:, half * LANES:(half + 1) * LANES]
            v2 = v_cols[:, half * LANES:(half + 1) * LANES]
            f_snd[h] = jnp.where(low, k2, roll_half(v2)).astype(BF16)
            f_snd[h + 1] = jnp.where(low, roll_half(k2), v2).astype(BF16)
            f_start(h)
            f_start(h + 1)
        return carry

    lax.fori_loop(0, blocks // 2, kv_block, 0)
    g_rcv[me] = g_snd[me]
    q_rcv[me] = q_snd[me]
    f_rcv[me] = f_snd[me]
    hall[core, me] = hp[2 * side + core]
    g_wait()
    q_wait()

    def turn_queries(i, carry):
        q2, g2 = q_rcv[i].astype(F32), g_rcv[i].astype(F32)
        both = jnp.concatenate(
            [jnp.where(low_half, q2, roll_half(g2)), jnp.where(low_half, roll_half(q2), g2)], axis=0
        )
        qg[i] = both.astype(BF16)
        qgt[:, lane_block(i)] = jnp.transpose(both).astype(BF16)
        return carry

    lax.fori_loop(0, n, turn_queries, 0)
    f_wait()
    h_start()

    def turn_keys(i, carry):
        kvt[:, lane_block(i)] = jnp.transpose(f_rcv[i].astype(F32)).astype(BF16)
        return carry

    lax.fori_loop(0, n, turn_keys, 0)

    q_rows = QB * rows
    q_low = lax.broadcasted_iota(I32, (q_rows, LANES), 1) < HD
    chunk_blocks = CHUNK // rows
    exp_scale = scale * math.log2(math.e)
    chunks = [slice(c * CHUNK, (c + 1) * CHUNK) for c in range(total // CHUNK)]

    def attend(i, carry):
        own = pl.ds(i * QB, QB)
        both = qg[own].reshape(q_rows, LANES)
        zero = jnp.zeros_like(both)
        q, g = jnp.where(q_low, both, zero), jnp.where(q_low, zero, both)
        q_pos = i * q_rows + lax.broadcasted_iota(I32, (q_rows, 1), 0)
        sq = utt_bounds(len_ref, q_pos)[0]
        tops = []
        for cols in chunks:
            s = jnp.where(sq == sk[0:1, cols], dot(q, kvt[:, cols]), -jnp.inf)
            s_ref[:, cols] = s
            tops.append(jnp.max(s, axis=1, keepdims=True))
        shift = functools.reduce(jnp.maximum, tops) * exp_scale
        sums = []
        for cols in chunks:
            e = jnp.exp2(s_ref[:, cols] * exp_scale - shift)
            s_ref[:, cols] = e
            sums.append(jnp.sum(e, axis=1, keepdims=True))
        inv = 1.0 / functools.reduce(jnp.add, sums)
        o = jnp.zeros((q_rows, LANES), F32)
        g_t = qgt[HD:LANES, lane_block(i, q_rows)]
        for c, cols in enumerate(chunks):
            probs = s_ref[:, cols] * inv
            s_ref[:, cols] = probs
            low_probs = probs.astype(BF16)
            these = slice(c * chunk_blocks, (c + 1) * chunk_blocks)
            o = o + dot(low_probs, f_rcv[these].reshape(CHUNK, LANES))
            acc[HD:LANES, cols] += dot(g_t, low_probs)
        rowdot = jnp.sum(g.astype(F32) * o, axis=1, keepdims=True)
        dq = jnp.zeros((q_rows, LANES), F32)
        q_t = qgt[0:HD, lane_block(i, q_rows)]
        for c, cols in enumerate(chunks):
            dscores = (s_ref[:, cols] * (dot(g, kvt[:, cols]) - rowdot)).astype(BF16)
            these = slice(c * chunk_blocks, (c + 1) * chunk_blocks)
            dq = dq + dot(dscores, f_rcv[these].reshape(CHUNK, LANES))
            acc[0:HD, cols] += dot(q_t, dscores)
        ad[own] = jnp.where(q_low, dq * scale, o).astype(BF16).reshape(QB, rows, LANES)
        for r in range(QB):
            ad_start(i * QB + r)
        return carry

    lax.fori_loop(0, n // QB, attend, 0)

    def turn_back(i, carry):
        cols = lane_block(i)
        both = jnp.concatenate([acc[0:HD, cols] * scale, acc[HD:LANES, cols]], axis=0)
        kvt2[side, :, cols] = both.astype(BF16)
        kv[i] = jnp.transpose(both).astype(BF16)
        kv_start(i)
        return carry

    lax.fori_loop(0, n, turn_back, 0)
    def swap(source, target, send, recv, peer):
        return pltpu.make_async_remote_copy(
            source, target, send, recv, device_id={"ctx": peer}, device_id_type=MESH
        )

    across_copy = swap(kvt2.at[side], kvt2.at[side], across_send, across_recv, across)
    across_arrival = swap(kvt2.at[1 - side], kvt2.at[1 - side], across_send, across_recv, across)
    mate_copy = swap(hall.at[core], hall.at[core], mate_send, mate_recv, mate)
    mate_arrival = swap(hall.at[1 - core], hall.at[1 - core], mate_send, mate_recv, mate)
    across_copy.start()
    h_wait()
    mate_copy.start()
    rad[me] = ad[me]
    rkv[me] = kv[me]

    ad_wait()

    def attended_block(p, carry):
        cols = lane_block(p)
        even, odd = rad[2 * p].astype(F32), rad[2 * p + 1].astype(F32)
        dquery = jnp.where(low, even, roll_half(odd))
        attended = jnp.where(low, roll_half(even), odd)
        out_ref[0, :, cols] = (hb[:, cols].astype(F32) + attended).astype(BF16)
        dh[p] = cot[:, cols].astype(F32) + dquery
        return carry

    lax.fori_loop(0, blocks, attended_block, 0)
    kv_wait()

    def grad_block(p, carry):
        even, odd = rkv[2 * p].astype(F32), rkv[2 * p + 1].astype(F32)
        kvg[:, lane_block(p)] = jnp.where(low, even, roll_half(odd)).astype(BF16)
        kvg[:, lane_block(p + blocks)] = jnp.where(low, roll_half(even), odd).astype(BF16)
        return carry

    lax.fori_loop(0, blocks, grad_block, 0)

    def dhidden_block(b, carry):
        back = dot_last(kvg[...], wkv[lane_block(b, 256), :])
        for half in range(2):
            p = 2 * b + half
            dhidden = dh[p] + back[:, half * LANES:(half + 1) * LANES]
            dh[p] = dhidden
            v = conv[p]
            s = 1.0 / (1.0 + jnp.exp(-v))
            dcb[:, lane_block(p)] = (dhidden * (s * (1.0 + v * (1.0 - s)))).astype(BF16)
        return carry

    lax.fori_loop(0, blocks // 2, dhidden_block, 0)

    halos2 = halo_copies(dcb, halo2, halo2_send, halo2_recv)
    for copy in halos2:
        copy.start()

    def tap_grads_block(b, carry):
        cols = lane_block(b)
        own = dcb[:, cols].astype(F32)
        pad[b, RIM:RIM + rows] = own
        for j in range(TAPS):
            a, r = divmod(j, 8)
            source = masked(taps_in(j, slice(0, rows)), xs[r, b, 8 * a:8 * a + rows])
            pdw[j:j + 1, cols] = jnp.sum(source * own, axis=0, keepdims=True)
        turned = jnp.transpose(pdw[:, cols])
        for half in range(2):
            packed = None
            for k in range(4):
                slab = turned[half * HD + 16 * k:half * HD + 16 * (k + 1)]
                slab = slab if k == 0 else pltpu.roll(slab, 32 * k, 1)
                packed = slab if packed is None else packed + slab
            w1s[2 * b + half] = packed
        return carry

    lax.fori_loop(0, blocks, tap_grads_block, 0)

    def w1_to(s):
        other = lax.rem(seq + s, m)
        return pltpu.make_async_remote_copy(
            w1s.at[other], w1r.at[seq], w1_send.at[other], w1_recv.at[seq],
            device_id={"dp": other}, device_id_type=MESH,
        )

    def w1_start(s, carry):
        w1_to(s).start()
        return carry

    lax.fori_loop(1, m, w1_start, 0)
    w1r[seq] = w1s[seq]

    mate_arrival.wait_recv()
    across_arrival.wait_recv()
    for k in range(2):
        part = jnp.transpose(dot(kvt2[...].reshape(2 * LANES, total), hall[k].reshape(total, width // 4)))
        for q in range(m // 4):
            for e in range(2):
                piece = part[q * HD:(q + 1) * HD, e * LANES:(e + 1) * LANES]
                g1s[2 * (k * (m // 4) + q) + e] = piece.astype(BF16)

    def g1_copy(index):
        q, e = lax.div(index, 2), lax.rem(index, 2)
        return pltpu.make_async_remote_copy(
            g1s.at[index], g1r.at[seq], g1_send.at[index], g1_recv.at[seq],
            device_id={"dp": 2 * q + side, "ctx": 4 * ring_spot + 2 * e + core}, device_id_type=MESH,
        )

    stays = lax.rem(seq, 2) == side
    own_piece = 2 * lax.div(seq, 2) + side

    def g1_start(index, carry):
        @pl.when(jnp.logical_not(stays & (index == own_piece)))
        def _():
            g1_copy(index).start()
        return carry

    lax.fori_loop(0, m, g1_start, 0)

    @pl.when(stays)
    def _():
        g1r[seq] = g1s[own_piece]

    for copy in halos2:
        copy.wait()

    def dframes_block(b, carry):
        cols = lane_block(b)
        pad[b, 0:RIM] = halo2[0, :, cols].astype(F32)
        pad[b, RIM + rows:2 * RIM + rows] = halo2[1, :, cols].astype(F32)
        for r in range(8):
            ys[r] = pad[b, r + 1:r + 1 + rows + 24]
        result = dh[b]
        for j in range(TAPS):
            a, r = divmod(j, 8)
            back = TAPS - 1 - j
            source = masked(taps_in(j, slice(0, rows)), ys[r, 8 * a:8 * a + rows])
            result = result + source * wdw[back:back + 1, cols]
        dfr_ref[0, :, cols] = result.astype(BF16)
        return carry

    lax.fori_loop(0, LATE, dframes_block, 0)

    def g1_wait(d, carry):
        @pl.when(jnp.logical_not((d == seq) & stays))
        def _():
            pltpu.make_async_remote_copy(
                g1s.at[0], g1r.at[d], g1_send.at[0], g1_recv.at[d],
                device_id={"ctx": mate}, device_id_type=MESH,
            ).wait_recv()
        return carry

    def w1_wait(s, carry):
        d = lax.rem(seq + s, m)
        pltpu.make_async_remote_copy(
            w1s.at[d], w1r.at[d], w1_send.at[d], w1_recv.at[d],
            device_id={"dp": d}, device_id_type=MESH,
        ).wait_recv()
        return carry

    lax.fori_loop(1, m, w1_wait, 0)
    lax.fori_loop(0, m, g1_wait, 0)
    kv_rows = functools.reduce(jnp.add, [g1r[d].astype(F32) for d in range(m)])
    dw_rows = functools.reduce(jnp.add, [w1r[d] for d in range(m)])
    for k in range(4):
        turned = dw_rows if k == 0 else pltpu.roll(dw_rows, LANES - 32 * k, 1)
        for r in range(4):
            c = 4 * k + r
            s2[c, 0:4] = kv_rows[4 * c:4 * c + 4]
            s2[c, 4:8] = turned[4 * r:4 * r + 4]
    t2_start()
    t2[me] = s2[me]

    lax.fori_loop(LATE, blocks, dframes_block, 0)

    g_sent()
    q_sent()
    f_sent()
    h_sent()
    ad_sent()
    kv_sent()
    mate_copy.wait_send()
    across_copy.wait_send()

    def g1_sent(index, carry):
        @pl.when(jnp.logical_not(stays & (index == own_piece)))
        def _():
            g1_copy(index).wait_send()
        return carry

    lax.fori_loop(0, m, g1_sent, 0)

    def w1_sent(s, carry):
        w1_to(s).wait_send()
        return carry

    lax.fori_loop(1, m, w1_sent, 0)
    t2_wait()
    low4 = lax.broadcasted_iota(I32, (4, LANES), 1) < HD
    for p in range(blocks):
        even, odd = t2[2 * p, 0:4], t2[2 * p + 1, 0:4]
        gkv_ref[:, p * LANES:(p + 1) * LANES] = jnp.where(low4, even, roll_half(odd))
        gkv_ref[:, width + p * LANES:width + (p + 1) * LANES] = jnp.where(low4, roll_half(even), odd)
    gdw_ref[...] = functools.reduce(jnp.add, [t2[h, 4:8] for h in range(n)])[:, 0:TAPS]
    t2_sent()


def hand_out(*refs):
    half = len(refs) // 2
    for source, target in zip(refs[:half], refs[half:]):
        target[...] = source[...]


def on_device(frames, utt_lengths, cotangent, w_dw, w_kv):
    n = lax.axis_size("ctx")
    rows, width = frames.shape[1], frames.shape[2]
    blocks = width // LANES
    total = n * rows
    dma = pltpu.SemaphoreType.DMA
    vmem = pltpu.VMEM
    scratch = [
        vmem((rows, width), BF16),
        vmem((rows, width), BF16),
        vmem(w_dw.shape, F32),
        vmem(w_kv.shape, BF16),
        vmem((2, RIM, width), BF16),
        vmem((2, RIM, width), BF16),
        vmem((blocks, rows + 2 * RIM, LANES), F32),
        vmem((8, blocks, rows + 24, LANES), F32),
        vmem((8, rows + 24, LANES), F32),
        vmem((rows, LANES), I32),
        vmem((rows, LANES), I32),
        vmem((blocks, rows, LANES), F32),
        vmem((rows, width), BF16),
        vmem((n, rows // 2, LANES), BF16),
        vmem((n, rows // 2, LANES), BF16),
        vmem((n, rows // 2, LANES), BF16),
        vmem((n, rows // 2, LANES), BF16),
        vmem((n, rows, LANES), BF16),
        vmem((n, rows, LANES), BF16),
        vmem((4, rows, width // 4), BF16),
        vmem((2, n, rows, width // 4), BF16),
        vmem((n, rows, LANES), BF16),
        vmem((LANES, total), BF16),
        vmem((LANES, total), BF16),
        vmem((8, total), I32),
        vmem((QB * rows, total), F32),
        vmem((LANES, total), F32),
        vmem((n, rows, LANES), BF16),
        vmem((n, rows, LANES), BF16),
        vmem((n, rows, LANES), BF16),
        vmem((n, rows, LANES), BF16),
        vmem((2, LANES, total), BF16),
        vmem((rows, 2 * width), BF16),
        vmem((blocks, rows, LANES), F32),
        vmem((rows, width), BF16),
        vmem((n, HD, LANES), BF16),
        vmem((n, HD, LANES), BF16),
        vmem((LANES, width), F32),
        vmem((n, 16, LANES), F32),
        vmem((n, 16, LANES), F32),
        vmem((n, 8, LANES), F32),
        vmem((n, 8, LANES), F32),
        dma((4,)), dma((2,)), dma((2,)), dma((2,)), dma((2,)),
        dma((n,)), dma((n,)), dma((n,)), dma((n,)), dma((n,)), dma((n,)), dma((n,)), dma((n,)),
        dma((n,)), dma((n,)), dma((n,)), dma((n,)), dma, dma, dma, dma, dma((n,)), dma((n,)),
        dma((n,)), dma((n,)), dma((n,)), dma((n,)),
    ]
    whole = pl.BlockSpec(memory_space=vmem)
    anywhere = pl.BlockSpec(memory_space=pl.ANY)
    results = (
        jax.ShapeDtypeStruct(frames.shape, BF16),
        jax.ShapeDtypeStruct(frames.shape, BF16),
        jax.ShapeDtypeStruct((4, 2 * width), F32),
        jax.ShapeDtypeStruct((4, TAPS), F32),
    )
    raw = pl.pallas_call(
        functools.partial(kernel, n),
        out_shape=results,
        in_specs=[pl.BlockSpec(memory_space=pltpu.SMEM), anywhere, anywhere, anywhere, anywhere],
        out_specs=(whole,) * 4,
        scratch_shapes=scratch,
        compiler_params=pltpu.CompilerParams(
            collective_id=0, has_side_effects=True, vmem_limit_bytes=56 << 20
        ),
    )(utt_lengths, frames, cotangent, w_dw, w_kv)
    return pl.pallas_call(
        hand_out, out_shape=results, in_specs=[whole] * 4, out_specs=(whole,) * 4,
        compiler_params=pltpu.CompilerParams(vmem_limit_bytes=4 << 20),
    )(*raw)


def solution(mesh):
    placed = (P("dp", "ctx", None), P("dp", None), P("dp", "ctx", None), P(), P())
    return jax.shard_map(
        on_device,
        mesh=mesh,
        in_specs=placed,
        out_specs=(
            P("dp", "ctx", None),
            P("dp", "ctx", None),
            P(("dp", "ctx"), None),
            P(("dp", "ctx"), None),
        ),
        check_vma=False,
    )
```

```python
import functools
import math

import jax
import jax.numpy as jnp
from jax import lax
from jax.experimental import pallas as pl
from jax.experimental.pallas import tpu as pltpu
from jax.sharding import PartitionSpec as P

F32, BF16, I32 = jnp.float32, jnp.bfloat16, jnp.int32
MESH = pl.DeviceIdType.MESH
HD = 64
LANES = 128
TAPS = 31
RIM = 16
FAR = 1 << 20
QB = 2
CHUNK = 1024
MOST = 1152
LATE = 5


def dot(a, b):
    return jnp.dot(a, b, preferred_element_type=F32)


def dot_last(a, b):
    return lax.dot_general(a, b, (((1,), (1,)), ((), ())), preferred_element_type=F32)


def lane_block(index, width=LANES):
    return pl.ds(pl.multiple_of(index * width, width), width)


def utt_bounds(len_ref, pos):
    end = jnp.int32(0)
    start_of = jnp.zeros(pos.shape, I32)
    end_of = jnp.full(pos.shape, FAR, I32)
    for u in range(len_ref.shape[1]):
        end = end + len_ref[0, u]
        start_of = jnp.where(end <= pos, end, start_of)
        end_of = jnp.minimum(end_of, jnp.where(end > pos, end, FAR))
    return start_of, end_of


def kernel(
    n,
    len_ref, fr_hbm, cot_hbm, wdw_hbm, wkv_hbm,
    out_ref, dfr_ref, gkv_ref, gdw_ref,
    fr, cot, wdw, wkv, halo, halo2, pad, xs, ys, jlo, jhi, conv, hb,
    g_snd, g_rcv, q_snd, q_rcv, f_snd, f_rcv, hp, hall,
    qg, qgt, kvt, sk, s_ref, acc, ad, kv, rad, rkv, kvt2,
    kvg, dh, dcb, g1s, g1r, pdw, w1s, w1r, s2, t2,
    local_sems, halo_send, halo_recv, halo2_send, halo2_recv,
    g_send, g_recv, q_send, q_recv, f_send, f_recv, h_send, h_recv,
    ad_send, ad_recv, kv_send, kv_recv, mate_send, mate_recv, across_send, across_recv, g1_send, g1_recv,
    w1_send, w1_recv, t2_send, t2_recv,
):
    rows, width = fr.shape
    blocks = width // LANES
    total = n * rows
    m = n
    me = lax.axis_index("ctx")
    seq = lax.axis_index("dp")
    core = lax.rem(me, 2)
    chip = lax.div(me, 2)
    mate = me + 1 - 2 * core
    side = lax.rem(chip, 2)
    across = me + 2 - 4 * side
    ring_spot = lax.div(chip, 2)
    scale = 1.0 / math.sqrt(HD)

    barrier = pltpu.get_barrier_semaphore()

    def greet_ctx(s, carry):
        pl.semaphore_signal(barrier, inc=1, device_id={"ctx": lax.rem(me + s, n)}, device_id_type=MESH)
        return carry

    def greet_dp(s, carry):
        other = lax.rem(seq + s, m)
        pl.semaphore_signal(barrier, inc=1, device_id={"dp": other}, device_id_type=MESH)
        pl.semaphore_signal(barrier, inc=1, device_id={"dp": other, "ctx": across}, device_id_type=MESH)
        return carry

    fr_copy = pltpu.make_async_copy(fr_hbm.at[0], fr, local_sems.at[0])
    wdw_copy = pltpu.make_async_copy(wdw_hbm, wdw, local_sems.at[1])
    cot_copy = pltpu.make_async_copy(cot_hbm.at[0], cot, local_sems.at[2])
    wkv_copy = pltpu.make_async_copy(wkv_hbm, wkv, local_sems.at[3])
    lax.fori_loop(1, m, greet_dp, 0)
    lax.fori_loop(1, n, greet_ctx, 0)
    for copy in (fr_copy, wdw_copy, cot_copy, wkv_copy):
        copy.start()

    low = lax.broadcasted_iota(I32, (rows, LANES), 1) < HD
    low_half = lax.broadcasted_iota(I32, (rows // 2, LANES), 1) < HD
    pos = me * rows + lax.broadcasted_iota(I32, (rows, LANES), 0)
    start_of, end_of = utt_bounds(len_ref, pos)
    jlo[...] = start_of - pos + TAPS // 2
    jhi[...] = end_of - pos + TAPS // 2

    def taps_in(j, part):
        if j < TAPS // 2:
            return j >= jlo[part]
        if j > TAPS // 2:
            return j < jhi[part]
        return None

    def masked(mask, value):
        return value if mask is None else jnp.where(mask, value, 0.0)

    def conv_part(b, first, last):
        cols = lane_block(b)
        part = slice(first, last)
        result = jnp.zeros((last - first, LANES), F32)
        for j in range(TAPS):
            a, r = divmod(j, 8)
            source = xs[r, b, 8 * a + first:8 * a + last]
            result = result + masked(taps_in(j, part), source) * wdw[j:j + 1, cols]
        conv[b, part] = result
        hidden = pad[b, RIM + first:RIM + last] + result / (1.0 + jnp.exp(-result))
        hb[part, cols] = hidden.astype(BF16)

    def conv_inner(b, carry):
        pad[b, RIM:RIM + rows] = fr[:, lane_block(b)].astype(F32)
        for r in range(8):
            xs[r, b, RIM:rows + 8] = pad[b, r + 1 + RIM:r + 1 + rows + 8]
        conv_part(b, RIM, rows - RIM)
        return carry

    def roll_half(x):
        return pltpu.roll(x, HD, 1)

    def split_heads(pair, target, p):
        top, bottom = pair[0:rows // 2], pair[rows // 2:]
        target[2 * p] = jnp.where(low_half, top, roll_half(bottom)).astype(BF16)
        target[2 * p + 1] = jnp.where(low_half, roll_half(top), bottom).astype(BF16)

    def pack_cotangent(p, carry):
        split_heads(cot[:, lane_block(p)].astype(F32), g_snd, p)
        return carry

    fr_copy.wait()
    wdw_copy.wait()
    pad[:, 0:RIM] = jnp.zeros((blocks, RIM, LANES), F32)
    pad[:, RIM + rows:2 * RIM + rows] = jnp.zeros((blocks, RIM, LANES), F32)
    lax.fori_loop(0, blocks, conv_inner, 0)
    cot_copy.wait()
    lax.fori_loop(0, blocks, pack_cotangent, 0)
    sk[...] = utt_bounds(len_ref, lax.broadcasted_iota(I32, (8, total), 1))[0]
    acc[...] = jnp.zeros(acc.shape, F32)
    pdw[...] = jnp.zeros(pdw.shape, F32)

    pl.semaphore_wait(barrier, (n - 1) + 2 * (m - 1))

    right, left = lax.rem(me + 1, n), lax.rem(me + n - 1, n)

    def halo_copies(source, target, send, recv):
        return (
            pltpu.make_async_remote_copy(
                source.at[pl.ds(rows - RIM, RIM)], target.at[0], send.at[0], recv.at[0],
                device_id={"ctx": right}, device_id_type=MESH,
            ),
            pltpu.make_async_remote_copy(
                source.at[pl.ds(0, RIM)], target.at[1], send.at[1], recv.at[1],
                device_id={"ctx": left}, device_id_type=MESH,
            ),
        )

    def exchange(source_of, target, send, recv):
        def copy_to(peer):
            return pltpu.make_async_remote_copy(
                source_of(peer), target(peer).at[me], send.at[peer], recv.at[me],
                device_id={"ctx": peer}, device_id_type=MESH,
            )

        def copy_from(peer):
            return pltpu.make_async_remote_copy(
                source_of(peer), target(me).at[peer], send.at[peer], recv.at[peer],
                device_id={"ctx": peer}, device_id_type=MESH,
            )

        def start(s, carry):
            copy_to(lax.rem(me + s, n)).start()
            return carry

        def start_one(peer):
            @pl.when(peer != me)
            def _():
                copy_to(peer).start()

        def wait_recv(s, carry):
            copy_from(lax.rem(me + n - s, n)).wait_recv()
            return carry

        def wait_send(s, carry):
            copy_to(lax.rem(me + s, n)).wait_send()
            return carry

        return (
            lambda first=1, last=n: lax.fori_loop(first, last, start, 0),
            start_one,
            lambda: lax.fori_loop(1, n, wait_recv, 0),
            lambda: lax.fori_loop(1, n, wait_send, 0),
        )

    g_start, _, g_wait, g_sent = exchange(lambda peer: g_snd.at[peer], lambda owner: g_rcv, g_send, g_recv)
    q_start, _, q_wait, q_sent = exchange(lambda peer: q_snd.at[peer], lambda owner: q_rcv, q_send, q_recv)
    _, f_start, f_wait, f_sent = exchange(lambda peer: f_snd.at[peer], lambda owner: f_rcv, f_send, f_recv)
    h_start, _, h_wait, h_sent = exchange(lambda peer: hp.at[lax.rem(peer, 4)], lambda owner: hall.at[lax.rem(owner, 2)], h_send, h_recv)
    _, ad_start, ad_wait, ad_sent = exchange(lambda peer: ad.at[peer], lambda owner: rad, ad_send, ad_recv)
    _, kv_start, kv_wait, kv_sent = exchange(lambda peer: kv.at[peer], lambda owner: rkv, kv_send, kv_recv)
    t2_start, _, t2_wait, t2_sent = exchange(lambda peer: s2.at[peer], lambda owner: t2, t2_send, t2_recv)

    halos = halo_copies(fr, halo, halo_send, halo_recv)
    for copy in halos:
        copy.start()
    g_start()
    for copy in halos:
        copy.wait()

    def conv_outer(b, carry):
        cols = lane_block(b)
        pad[b, 0:RIM] = halo[0, :, cols].astype(F32)
        pad[b, RIM + rows:2 * RIM + rows] = halo[1, :, cols].astype(F32)
        for r in range(8):
            xs[r, b, 0:RIM] = pad[b, r + 1:r + 1 + RIM]
            xs[r, b, rows + 8:rows + 24] = pad[b, r + 9 + rows:r + 25 + rows]
        conv_part(b, 0, RIM)
        conv_part(b, rows - RIM, rows)
        return carry

    lax.fori_loop(0, blocks, conv_outer, 0)

    def pack_hidden(b, carry):
        first, second = [hb[:, lane_block(2 * b + k)].astype(F32) for k in range(2)]
        split_heads(first, q_snd, 2 * b)
        split_heads(second, q_snd, 2 * b + 1)
        part = lane_block(lax.rem(b, 2))
        hp[lax.div(b, 2), :, part] = jnp.where(low, first, roll_half(second)).astype(BF16)
        hp[2 + lax.div(b, 2), :, part] = jnp.where(low, roll_half(first), second).astype(BF16)
        return carry

    lax.fori_loop(0, blocks // 2, pack_hidden, 0)
    q_start()
    wkv_copy.wait()

    def kv_block(b, carry):
        k_cols = dot(hb[...], wkv[:, lane_block(b, 256)])
        v_cols = dot(hb[...], wkv[:, lane_block(b + blocks // 2, 256)])
        for half in range(2):
            h = 2 * (2 * b + half)
            k2 = k_cols[:, half * LANES:(half + 1) * LANES]
            v2 = v_cols[:, half * LANES:(half + 1) * LANES]
            f_snd[h] = jnp.where(low, k2, roll_half(v2)).astype(BF16)
            f_snd[h + 1] = jnp.where(low, roll_half(k2), v2).astype(BF16)
            f_start(h)
            f_start(h + 1)
        return carry

    lax.fori_loop(0, blocks // 2, kv_block, 0)
    g_rcv[me] = g_snd[me]
    q_rcv[me] = q_snd[me]
    f_rcv[me] = f_snd[me]
    hall[core, me] = hp[2 * side + core]
    g_wait()
    q_wait()

    def turn_queries(i, carry):
        q2, g2 = q_rcv[i].astype(F32), g_rcv[i].astype(F32)
        both = jnp.concatenate(
            [jnp.where(low_half, q2, roll_half(g2)), jnp.where(low_half, roll_half(q2), g2)], axis=0
        )
        qg[i] = both.astype(BF16)
        qgt[:, lane_block(i)] = jnp.transpose(both).astype(BF16)
        return carry

    lax.fori_loop(0, n, turn_queries, 0)
    f_wait()
    h_start()

    def turn_keys(i, carry):
        kvt[:, lane_block(i)] = jnp.transpose(f_rcv[i].astype(F32)).astype(BF16)
        return carry

    lax.fori_loop(0, n, turn_keys, 0)

    q_rows = QB * rows
    q_low = lax.broadcasted_iota(I32, (q_rows, LANES), 1) < HD
    exp_scale = scale * math.log2(math.e)

    def first_key(i):
        return min(max(0, i * q_rows - (MOST - 1)) // rows * rows, total)

    def last_key(i):
        return min(total, -(-((i + 1) * q_rows - 1 + MOST) // rows) * rows)

    def attend(i):
        own = slice(i * QB, (i + 1) * QB)
        edges = sorted({first_key(i), min(first_key(i) + CHUNK, last_key(i)), last_key(i)})
        chunks = [slice(a, b) for a, b in zip(edges[:-1], edges[1:])]

        def keys_of(cols):
            return f_rcv[cols.start // rows:cols.stop // rows].reshape(cols.stop - cols.start, LANES)

        both = qg[own].reshape(q_rows, LANES)
        zero = jnp.zeros_like(both)
        q, g = jnp.where(q_low, both, zero), jnp.where(q_low, zero, both)
        q_pos = i * q_rows + lax.broadcasted_iota(I32, (q_rows, 1), 0)
        sq = utt_bounds(len_ref, q_pos)[0]
        tops = []
        for cols in chunks:
            s = jnp.where(sq == sk[0:1, cols], dot(q, kvt[:, cols]), -jnp.inf)
            s_ref[:, cols] = s
            tops.append(jnp.max(s, axis=1, keepdims=True))
        shift = functools.reduce(jnp.maximum, tops) * exp_scale
        sums = []
        for cols in chunks:
            e = jnp.exp2(s_ref[:, cols] * exp_scale - shift)
            s_ref[:, cols] = e
            sums.append(jnp.sum(e, axis=1, keepdims=True))
        inv = 1.0 / functools.reduce(jnp.add, sums)
        o = jnp.zeros((q_rows, LANES), F32)
        g_t = qgt[HD:LANES, i * q_rows:(i + 1) * q_rows]
        for cols in chunks:
            probs = s_ref[:, cols] * inv
            s_ref[:, cols] = probs
            low_probs = probs.astype(BF16)
            o = o + dot(low_probs, keys_of(cols))
            acc[HD:LANES, cols] += dot(g_t, low_probs)
        rowdot = jnp.sum(g.astype(F32) * o, axis=1, keepdims=True)
        dq = jnp.zeros((q_rows, LANES), F32)
        q_t = qgt[0:HD, i * q_rows:(i + 1) * q_rows]
        for cols in chunks:
            dscores = (s_ref[:, cols] * (dot(g, kvt[:, cols]) - rowdot)).astype(BF16)
            dq = dq + dot(dscores, keys_of(cols))
            acc[0:HD, cols] += dot(q_t, dscores)
        ad[own] = jnp.where(q_low, dq * scale, o).astype(BF16).reshape(QB, rows, LANES)
        for r in range(QB):
            ad_start(i * QB + r)

    def turn_back(i, carry):
        cols = lane_block(i)
        both = jnp.concatenate([acc[0:HD, cols] * scale, acc[HD:LANES, cols]], axis=0)
        kvt2[side, :, cols] = both.astype(BF16)
        kv[i] = jnp.transpose(both).astype(BF16)
        kv_start(i)
        return carry

    def swap(source, target, send, recv, peer):
        return pltpu.make_async_remote_copy(
            source, target, send, recv, device_id={"ctx": peer}, device_id_type=MESH
        )

    steps = n // QB
    early = first_key(steps - 1)
    spans = [slice(0, early), slice(early, total)]

    def across_part(k, who):
        part = kvt2.at[who, :, spans[k]]
        return swap(part, part, across_send.at[k], across_recv.at[k], across)

    mate_copy = swap(hall.at[core], hall.at[core], mate_send, mate_recv, mate)
    mate_arrival = swap(hall.at[1 - core], hall.at[1 - core], mate_send, mate_recv, mate)

    for i in range(steps):
        attend(i)
        final = total if i == steps - 1 else first_key(i + 1)
        lax.fori_loop(first_key(i) // rows, final // rows, turn_back, 0)
        if i == steps - 2:
            across_part(0, side).start()
            h_wait()
            mate_copy.start()
    across_part(1, side).start()
    rad[me] = ad[me]
    rkv[me] = kv[me]

    ad_wait()

    def attended_block(p, carry):
        cols = lane_block(p)
        even, odd = rad[2 * p].astype(F32), rad[2 * p + 1].astype(F32)
        dquery = jnp.where(low, even, roll_half(odd))
        attended = jnp.where(low, roll_half(even), odd)
        out_ref[0, :, cols] = (hb[:, cols].astype(F32) + attended).astype(BF16)
        dh[p] = cot[:, cols].astype(F32) + dquery
        return carry

    lax.fori_loop(0, blocks, attended_block, 0)
    kv_wait()

    def grad_block(p, carry):
        even, odd = rkv[2 * p].astype(F32), rkv[2 * p + 1].astype(F32)
        kvg[:, lane_block(p)] = jnp.where(low, even, roll_half(odd)).astype(BF16)
        kvg[:, lane_block(p + blocks)] = jnp.where(low, roll_half(even), odd).astype(BF16)
        return carry

    lax.fori_loop(0, blocks, grad_block, 0)

    def dhidden_block(b, carry):
        back = dot_last(kvg[...], wkv[lane_block(b, 256), :])
        for half in range(2):
            p = 2 * b + half
            dhidden = dh[p] + back[:, half * LANES:(half + 1) * LANES]
            dh[p] = dhidden
            v = conv[p]
            s = 1.0 / (1.0 + jnp.exp(-v))
            dcb[:, lane_block(p)] = (dhidden * (s * (1.0 + v * (1.0 - s)))).astype(BF16)
        return carry

    lax.fori_loop(0, blocks // 2, dhidden_block, 0)

    halos2 = halo_copies(dcb, halo2, halo2_send, halo2_recv)
    for copy in halos2:
        copy.start()

    def tap_grads_block(b, carry):
        cols = lane_block(b)
        own = dcb[:, cols].astype(F32)
        pad[b, RIM:RIM + rows] = own
        for j in range(TAPS):
            a, r = divmod(j, 8)
            source = masked(taps_in(j, slice(0, rows)), xs[r, b, 8 * a:8 * a + rows])
            pdw[j:j + 1, cols] = jnp.sum(source * own, axis=0, keepdims=True)
        turned = jnp.transpose(pdw[:, cols])
        for half in range(2):
            packed = None
            for k in range(4):
                slab = turned[half * HD + 16 * k:half * HD + 16 * (k + 1)]
                slab = slab if k == 0 else pltpu.roll(slab, 32 * k, 1)
                packed = slab if packed is None else packed + slab
            w1s[2 * b + half] = packed
        return carry

    lax.fori_loop(0, blocks, tap_grads_block, 0)

    def w1_to(s):
        other = lax.rem(seq + s, m)
        return pltpu.make_async_remote_copy(
            w1s.at[other], w1r.at[seq], w1_send.at[other], w1_recv.at[seq],
            device_id={"dp": other}, device_id_type=MESH,
        )

    def w1_start(s, carry):
        w1_to(s).start()
        return carry

    lax.fori_loop(1, m, w1_start, 0)
    w1r[seq] = w1s[seq]

    mate_arrival.wait_recv()
    for k in range(2):
        across_part(k, 1 - side).wait_recv()
    for k in range(2):
        part = jnp.transpose(dot(kvt2[...].reshape(2 * LANES, total), hall[k].reshape(total, width // 4)))
        for q in range(m // 4):
            for e in range(2):
                piece = part[q * HD:(q + 1) * HD, e * LANES:(e + 1) * LANES]
                g1s[2 * (k * (m // 4) + q) + e] = piece.astype(BF16)

    def g1_copy(index):
        q, e = lax.div(index, 2), lax.rem(index, 2)
        return pltpu.make_async_remote_copy(
            g1s.at[index], g1r.at[seq], g1_send.at[index], g1_recv.at[seq],
            device_id={"dp": 2 * q + side, "ctx": 4 * ring_spot + 2 * e + core}, device_id_type=MESH,
        )

    stays = lax.rem(seq, 2) == side
    own_piece = 2 * lax.div(seq, 2) + side

    def g1_start(index, carry):
        @pl.when(jnp.logical_not(stays & (index == own_piece)))
        def _():
            g1_copy(index).start()
        return carry

    lax.fori_loop(0, m, g1_start, 0)

    @pl.when(stays)
    def _():
        g1r[seq] = g1s[own_piece]

    for copy in halos2:
        copy.wait()

    def dframes_block(b, carry):
        cols = lane_block(b)
        pad[b, 0:RIM] = halo2[0, :, cols].astype(F32)
        pad[b, RIM + rows:2 * RIM + rows] = halo2[1, :, cols].astype(F32)
        for r in range(8):
            ys[r] = pad[b, r + 1:r + 1 + rows + 24]
        result = dh[b]
        for j in range(TAPS):
            a, r = divmod(j, 8)
            back = TAPS - 1 - j
            source = masked(taps_in(j, slice(0, rows)), ys[r, 8 * a:8 * a + rows])
            result = result + source * wdw[back:back + 1, cols]
        dfr_ref[0, :, cols] = result.astype(BF16)
        return carry

    lax.fori_loop(0, LATE, dframes_block, 0)

    def g1_wait(d, carry):
        @pl.when(jnp.logical_not((d == seq) & stays))
        def _():
            pltpu.make_async_remote_copy(
                g1s.at[0], g1r.at[d], g1_send.at[0], g1_recv.at[d],
                device_id={"ctx": mate}, device_id_type=MESH,
            ).wait_recv()
        return carry

    def w1_wait(s, carry):
        d = lax.rem(seq + s, m)
        pltpu.make_async_remote_copy(
            w1s.at[d], w1r.at[d], w1_send.at[d], w1_recv.at[d],
            device_id={"dp": d}, device_id_type=MESH,
        ).wait_recv()
        return carry

    lax.fori_loop(1, m, w1_wait, 0)
    lax.fori_loop(0, m, g1_wait, 0)
    kv_rows = functools.reduce(jnp.add, [g1r[d].astype(F32) for d in range(m)])
    dw_rows = functools.reduce(jnp.add, [w1r[d] for d in range(m)])
    for k in range(4):
        turned = dw_rows if k == 0 else pltpu.roll(dw_rows, LANES - 32 * k, 1)
        for r in range(4):
            c = 4 * k + r
            s2[c, 0:4] = kv_rows[4 * c:4 * c + 4]
            s2[c, 4:8] = turned[4 * r:4 * r + 4]
    t2_start()
    t2[me] = s2[me]

    lax.fori_loop(LATE, blocks, dframes_block, 0)

    g_sent()
    q_sent()
    f_sent()
    h_sent()
    ad_sent()
    kv_sent()
    mate_copy.wait_send()
    for k in range(2):
        across_part(k, side).wait_send()

    def g1_sent(index, carry):
        @pl.when(jnp.logical_not(stays & (index == own_piece)))
        def _():
            g1_copy(index).wait_send()
        return carry

    lax.fori_loop(0, m, g1_sent, 0)

    def w1_sent(s, carry):
        w1_to(s).wait_send()
        return carry

    lax.fori_loop(1, m, w1_sent, 0)
    t2_wait()
    low4 = lax.broadcasted_iota(I32, (4, LANES), 1) < HD
    for p in range(blocks):
        even, odd = t2[2 * p, 0:4], t2[2 * p + 1, 0:4]
        gkv_ref[:, p * LANES:(p + 1) * LANES] = jnp.where(low4, even, roll_half(odd))
        gkv_ref[:, width + p * LANES:width + (p + 1) * LANES] = jnp.where(low4, roll_half(even), odd)
    gdw_ref[...] = functools.reduce(jnp.add, [t2[h, 4:8] for h in range(n)])[:, 0:TAPS]
    t2_sent()


def hand_out(*refs):
    sources, targets, stages, sems = refs[:4], refs[4:8], refs[8:12], refs[12]
    loads = [pltpu.make_async_copy(a, b, sems.at[0, k]) for k, (a, b) in enumerate(zip(sources, stages))]
    stores = [pltpu.make_async_copy(a, b, sems.at[1, k]) for k, (a, b) in enumerate(zip(stages, targets))]
    for load in loads:
        load.start()
    for load, store in zip(loads, stores):
        load.wait()
        store.start()
    for store in stores:
        store.wait()


def on_device(frames, utt_lengths, cotangent, w_dw, w_kv):
    n = lax.axis_size("ctx")
    rows, width = frames.shape[1], frames.shape[2]
    blocks = width // LANES
    total = n * rows
    dma = pltpu.SemaphoreType.DMA
    vmem = pltpu.VMEM
    scratch = [
        vmem((rows, width), BF16),
        vmem((rows, width), BF16),
        vmem(w_dw.shape, F32),
        vmem(w_kv.shape, BF16),
        vmem((2, RIM, width), BF16),
        vmem((2, RIM, width), BF16),
        vmem((blocks, rows + 2 * RIM, LANES), F32),
        vmem((8, blocks, rows + 24, LANES), F32),
        vmem((8, rows + 24, LANES), F32),
        vmem((rows, LANES), I32),
        vmem((rows, LANES), I32),
        vmem((blocks, rows, LANES), F32),
        vmem((rows, width), BF16),
        vmem((n, rows // 2, LANES), BF16),
        vmem((n, rows // 2, LANES), BF16),
        vmem((n, rows // 2, LANES), BF16),
        vmem((n, rows // 2, LANES), BF16),
        vmem((n, rows, LANES), BF16),
        vmem((n, rows, LANES), BF16),
        vmem((4, rows, width // 4), BF16),
        vmem((2, n, rows, width // 4), BF16),
        vmem((n, rows, LANES), BF16),
        vmem((LANES, total), BF16),
        vmem((LANES, total), BF16),
        vmem((8, total), I32),
        vmem((QB * rows, total), F32),
        vmem((LANES, total), F32),
        vmem((n, rows, LANES), BF16),
        vmem((n, rows, LANES), BF16),
        vmem((n, rows, LANES), BF16),
        vmem((n, rows, LANES), BF16),
        vmem((2, LANES, total), BF16),
        vmem((rows, 2 * width), BF16),
        vmem((blocks, rows, LANES), F32),
        vmem((rows, width), BF16),
        vmem((n, HD, LANES), BF16),
        vmem((n, HD, LANES), BF16),
        vmem((LANES, width), F32),
        vmem((n, 16, LANES), F32),
        vmem((n, 16, LANES), F32),
        vmem((n, 8, LANES), F32),
        vmem((n, 8, LANES), F32),
        dma((4,)), dma((2,)), dma((2,)), dma((2,)), dma((2,)),
        dma((n,)), dma((n,)), dma((n,)), dma((n,)), dma((n,)), dma((n,)), dma((n,)), dma((n,)),
        dma((n,)), dma((n,)), dma((n,)), dma((n,)), dma, dma, dma((2,)), dma((2,)), dma((n,)), dma((n,)),
        dma((n,)), dma((n,)), dma((n,)), dma((n,)),
    ]
    whole = pl.BlockSpec(memory_space=vmem)
    anywhere = pl.BlockSpec(memory_space=pl.ANY)
    in_hbm = pl.BlockSpec(memory_space=pltpu.HBM)
    results = (
        jax.ShapeDtypeStruct(frames.shape, BF16),
        jax.ShapeDtypeStruct(frames.shape, BF16),
        jax.ShapeDtypeStruct((4, 2 * width), F32),
        jax.ShapeDtypeStruct((4, TAPS), F32),
    )
    raw = pl.pallas_call(
        functools.partial(kernel, n),
        out_shape=results,
        in_specs=[pl.BlockSpec(memory_space=pltpu.SMEM), anywhere, anywhere, anywhere, anywhere],
        out_specs=(whole,) * 4,
        scratch_shapes=scratch,
        compiler_params=pltpu.CompilerParams(
            collective_id=0, has_side_effects=True, vmem_limit_bytes=56 << 20
        ),
    )(utt_lengths, frames, cotangent, w_dw, w_kv)
    return pl.pallas_call(
        hand_out, out_shape=results, in_specs=[in_hbm] * 4, out_specs=(in_hbm,) * 4,
        scratch_shapes=[vmem(r.shape, r.dtype) for r in results] + [dma((2, 4))],
    )(*raw)


def solution(mesh):
    placed = (P("dp", "ctx", None), P("dp", None), P("dp", "ctx", None), P(), P())
    return jax.shard_map(
        on_device,
        mesh=mesh,
        in_specs=placed,
        out_specs=(
            P("dp", "ctx", None),
            P("dp", "ctx", None),
            P(("dp", "ctx"), None),
            P(("dp", "ctx"), None),
        ),
        check_vma=False,
    )
```

```python
import functools
import math

import jax
import jax.numpy as jnp
from jax import lax
from jax.experimental import pallas as pl
from jax.experimental.pallas import tpu as pltpu
from jax.sharding import PartitionSpec as P

F32, BF16, I32 = jnp.float32, jnp.bfloat16, jnp.int32
MESH = pl.DeviceIdType.MESH
HD = 64
LANES = 128
TAPS = 31
RIM = 16
FAR = 1 << 20
QB = 2
MOST = 1152
LATE = 6


def dot(a, b):
    return jnp.dot(a, b, preferred_element_type=F32)


def dot_last(a, b):
    return lax.dot_general(a, b, (((1,), (1,)), ((), ())), preferred_element_type=F32)


def lane_block(index, width=LANES):
    return pl.ds(pl.multiple_of(index * width, width), width)


def utt_bounds(len_ref, pos):
    end = jnp.int32(0)
    start_of = jnp.zeros(pos.shape, I32)
    end_of = jnp.full(pos.shape, FAR, I32)
    for u in range(len_ref.shape[1]):
        end = end + len_ref[0, u]
        start_of = jnp.where(end <= pos, end, start_of)
        end_of = jnp.minimum(end_of, jnp.where(end > pos, end, FAR))
    return start_of, end_of


def kernel(
    n,
    len_ref, fr_hbm, cot_hbm, wdw_hbm, wkv_hbm,
    out_ref, dfr_ref, gkv_ref, gdw_ref,
    fr, cot, wdw, wkv, halo, halo2, pad, xs, ys, jlo, jhi, conv, hb,
    g_snd, g_rcv, q_snd, q_rcv, f_snd, f_rcv, hp, hall,
    qg, qgt, kvt, sk, s_ref, acc, ad, kv, rad, rkv, kvt2,
    kvg, dh, dcb, g1s, g1r, pdw, w1s, w1r, s2, t2,
    local_sems, halo_send, halo_recv, halo2_send, halo2_recv,
    g_send, g_recv, q_send, q_recv, f_send, f_recv, h_send, h_recv,
    ad_send, ad_recv, kv_send, kv_recv, mate_send, mate_recv, across_send, across_recv, g1_send, g1_recv,
    w1_send, w1_recv, t2_send, t2_recv,
):
    rows, width = fr.shape
    blocks = width // LANES
    total = n * rows
    m = n
    me = lax.axis_index("ctx")
    seq = lax.axis_index("dp")
    core = lax.rem(me, 2)
    chip = lax.div(me, 2)
    mate = me + 1 - 2 * core
    side = lax.rem(chip, 2)
    across = me + 2 - 4 * side
    ring_spot = lax.div(chip, 2)
    scale = 1.0 / math.sqrt(HD)

    barrier = pltpu.get_barrier_semaphore()

    def greet_ctx(s, carry):
        pl.semaphore_signal(barrier, inc=1, device_id={"ctx": lax.rem(me + s, n)}, device_id_type=MESH)
        return carry

    def greet_dp(s, carry):
        other = lax.rem(seq + s, m)
        pl.semaphore_signal(barrier, inc=1, device_id={"dp": other}, device_id_type=MESH)
        pl.semaphore_signal(barrier, inc=1, device_id={"dp": other, "ctx": across}, device_id_type=MESH)
        return carry

    fr_copy = pltpu.make_async_copy(fr_hbm.at[0], fr, local_sems.at[0])
    wdw_copy = pltpu.make_async_copy(wdw_hbm, wdw, local_sems.at[1])
    cot_copy = pltpu.make_async_copy(cot_hbm.at[0], cot, local_sems.at[2])
    wkv_copy = pltpu.make_async_copy(wkv_hbm, wkv, local_sems.at[3])
    lax.fori_loop(1, m, greet_dp, 0)
    lax.fori_loop(1, n, greet_ctx, 0)
    for copy in (fr_copy, wdw_copy, cot_copy, wkv_copy):
        copy.start()

    low = lax.broadcasted_iota(I32, (rows, LANES), 1) < HD
    low_half = lax.broadcasted_iota(I32, (rows // 2, LANES), 1) < HD
    pos = me * rows + lax.broadcasted_iota(I32, (rows, LANES), 0)
    start_of, end_of = utt_bounds(len_ref, pos)
    jlo[...] = start_of - pos + TAPS // 2
    jhi[...] = end_of - pos + TAPS // 2

    def taps_in(j, part):
        if j < TAPS // 2:
            return j >= jlo[part]
        if j > TAPS // 2:
            return j < jhi[part]
        return None

    def masked(mask, value):
        return value if mask is None else jnp.where(mask, value, 0.0)

    def conv_part(b, first, last):
        cols = lane_block(b)
        part = slice(first, last)
        result = jnp.zeros((last - first, LANES), F32)
        for j in range(TAPS):
            a, r = divmod(j, 8)
            source = xs[r, b, 8 * a + first:8 * a + last]
            result = result + masked(taps_in(j, part), source) * wdw[j:j + 1, cols]
        conv[b, part] = result
        hidden = pad[b, RIM + first:RIM + last] + result / (1.0 + jnp.exp(-result))
        hb[part, cols] = hidden.astype(BF16)

    def conv_inner(b, carry):
        pad[b, RIM:RIM + rows] = fr[:, lane_block(b)].astype(F32)
        for r in range(8):
            xs[r, b, RIM:rows + 8] = pad[b, r + 1 + RIM:r + 1 + rows + 8]
        conv_part(b, RIM, rows - RIM)
        return carry

    def roll_half(x):
        return pltpu.roll(x, HD, 1)

    def split_heads(pair, target, p):
        top, bottom = pair[0:rows // 2], pair[rows // 2:]
        target[2 * p] = jnp.where(low_half, top, roll_half(bottom)).astype(BF16)
        target[2 * p + 1] = jnp.where(low_half, roll_half(top), bottom).astype(BF16)

    def pack_cotangent(p, carry):
        split_heads(cot[:, lane_block(p)].astype(F32), g_snd, p)
        return carry

    fr_copy.wait()
    wdw_copy.wait()
    pad[:, 0:RIM] = jnp.zeros((blocks, RIM, LANES), F32)
    pad[:, RIM + rows:2 * RIM + rows] = jnp.zeros((blocks, RIM, LANES), F32)
    lax.fori_loop(0, blocks, conv_inner, 0)
    cot_copy.wait()
    lax.fori_loop(0, blocks, pack_cotangent, 0)
    sk[...] = utt_bounds(len_ref, lax.broadcasted_iota(I32, (8, total), 1))[0]
    acc[...] = jnp.zeros(acc.shape, F32)
    pdw[...] = jnp.zeros(pdw.shape, F32)

    pl.semaphore_wait(barrier, (n - 1) + 2 * (m - 1))

    right, left = lax.rem(me + 1, n), lax.rem(me + n - 1, n)

    def halo_copies(source, target, send, recv):
        return (
            pltpu.make_async_remote_copy(
                source.at[pl.ds(rows - RIM, RIM)], target.at[0], send.at[0], recv.at[0],
                device_id={"ctx": right}, device_id_type=MESH,
            ),
            pltpu.make_async_remote_copy(
                source.at[pl.ds(0, RIM)], target.at[1], send.at[1], recv.at[1],
                device_id={"ctx": left}, device_id_type=MESH,
            ),
        )

    def exchange(source_of, target, send, recv):
        def copy_to(peer):
            return pltpu.make_async_remote_copy(
                source_of(peer), target(peer).at[me], send.at[peer], recv.at[me],
                device_id={"ctx": peer}, device_id_type=MESH,
            )

        def copy_from(peer):
            return pltpu.make_async_remote_copy(
                source_of(peer), target(me).at[peer], send.at[peer], recv.at[peer],
                device_id={"ctx": peer}, device_id_type=MESH,
            )

        def start(s, carry):
            copy_to(lax.rem(me + s, n)).start()
            return carry

        def start_one(peer):
            @pl.when(peer != me)
            def _():
                copy_to(peer).start()

        def wait_recv(s, carry):
            copy_from(lax.rem(me + n - s, n)).wait_recv()
            return carry

        def wait_send(s, carry):
            copy_to(lax.rem(me + s, n)).wait_send()
            return carry

        return (
            lambda first=1, last=n: lax.fori_loop(first, last, start, 0),
            start_one,
            lambda: lax.fori_loop(1, n, wait_recv, 0),
            lambda: lax.fori_loop(1, n, wait_send, 0),
        )

    g_start, _, g_wait, g_sent = exchange(lambda peer: g_snd.at[peer], lambda owner: g_rcv, g_send, g_recv)
    q_start, _, q_wait, q_sent = exchange(lambda peer: q_snd.at[peer], lambda owner: q_rcv, q_send, q_recv)
    _, f_start, f_wait, f_sent = exchange(lambda peer: f_snd.at[peer], lambda owner: f_rcv, f_send, f_recv)
    h_start, _, h_wait, h_sent = exchange(lambda peer: hp.at[lax.rem(peer, 4)], lambda owner: hall.at[lax.rem(owner, 2)], h_send, h_recv)
    _, ad_start, ad_wait, ad_sent = exchange(lambda peer: ad.at[peer], lambda owner: rad, ad_send, ad_recv)
    _, kv_start, kv_wait, kv_sent = exchange(lambda peer: kv.at[peer], lambda owner: rkv, kv_send, kv_recv)
    t2_start, _, t2_wait, t2_sent = exchange(lambda peer: s2.at[peer], lambda owner: t2, t2_send, t2_recv)

    halos = halo_copies(fr, halo, halo_send, halo_recv)
    for copy in halos:
        copy.start()
    g_start()
    for copy in halos:
        copy.wait()

    def conv_outer(b, carry):
        cols = lane_block(b)
        pad[b, 0:RIM] = halo[0, :, cols].astype(F32)
        pad[b, RIM + rows:2 * RIM + rows] = halo[1, :, cols].astype(F32)
        for r in range(8):
            xs[r, b, 0:RIM] = pad[b, r + 1:r + 1 + RIM]
            xs[r, b, rows + 8:rows + 24] = pad[b, r + 9 + rows:r + 25 + rows]
        conv_part(b, 0, RIM)
        conv_part(b, rows - RIM, rows)
        return carry

    lax.fori_loop(0, blocks, conv_outer, 0, unroll=4)

    def pack_hidden(b, carry):
        first, second = [hb[:, lane_block(2 * b + k)].astype(F32) for k in range(2)]
        split_heads(first, q_snd, 2 * b)
        split_heads(second, q_snd, 2 * b + 1)
        return carry

    def pack_gather(b, carry):
        first, second = [hb[:, lane_block(2 * b + k)].astype(F32) for k in range(2)]
        part = lane_block(lax.rem(b, 2))
        hp[lax.div(b, 2), :, part] = jnp.where(low, first, roll_half(second)).astype(BF16)
        hp[2 + lax.div(b, 2), :, part] = jnp.where(low, roll_half(first), second).astype(BF16)
        return carry

    lax.fori_loop(0, blocks // 2, pack_hidden, 0, unroll=2)
    q_start()
    wkv_copy.wait()

    def kv_block(b, carry):
        k_cols = dot(hb[...], wkv[:, lane_block(b, 256)])
        v_cols = dot(hb[...], wkv[:, lane_block(b + blocks // 2, 256)])
        for half in range(2):
            h = 2 * (2 * b + half)
            k2 = k_cols[:, half * LANES:(half + 1) * LANES]
            v2 = v_cols[:, half * LANES:(half + 1) * LANES]
            f_snd[h] = jnp.where(low, k2, roll_half(v2)).astype(BF16)
            f_snd[h + 1] = jnp.where(low, roll_half(k2), v2).astype(BF16)
            f_start(h)
            f_start(h + 1)
        return carry

    lax.fori_loop(0, blocks // 2, kv_block, 0, unroll=2)
    lax.fori_loop(0, blocks // 2, pack_gather, 0)
    g_rcv[me] = g_snd[me]
    q_rcv[me] = q_snd[me]
    f_rcv[me] = f_snd[me]
    hall[core, me] = hp[2 * side + core]
    g_wait()
    q_wait()

    def turn_queries(i, carry):
        q2, g2 = q_rcv[i].astype(F32), g_rcv[i].astype(F32)
        both = jnp.concatenate(
            [jnp.where(low_half, q2, roll_half(g2)), jnp.where(low_half, roll_half(q2), g2)], axis=0
        )
        qg[i] = both.astype(BF16)
        qgt[:, lane_block(i)] = jnp.transpose(both).astype(BF16)
        return carry

    lax.fori_loop(0, n, turn_queries, 0, unroll=4)
    f_wait()
    h_start()

    def turn_keys(i, carry):
        kvt[:, lane_block(i)] = jnp.transpose(f_rcv[i].astype(F32)).astype(BF16)
        return carry

    lax.fori_loop(0, n, turn_keys, 0, unroll=4)

    q_rows = QB * rows
    q_low = lax.broadcasted_iota(I32, (q_rows, LANES), 1) < HD
    exp_scale = scale * math.log2(math.e)

    def first_key(i):
        return min(max(0, i * q_rows - (MOST - 1)) // rows * rows, total)

    def last_key(i):
        return min(total, -(-((i + 1) * q_rows - 1 + MOST) // rows) * rows)

    def attend(i):
        own = slice(i * QB, (i + 1) * QB)
        chunks = [slice(first_key(i), last_key(i))]

        def keys_of(cols):
            return f_rcv[cols.start // rows:cols.stop // rows].reshape(cols.stop - cols.start, LANES)

        both = qg[own].reshape(q_rows, LANES)
        zero = jnp.zeros_like(both)
        q, g = jnp.where(q_low, both, zero), jnp.where(q_low, zero, both)
        q_pos = i * q_rows + lax.broadcasted_iota(I32, (q_rows, 1), 0)
        sq = utt_bounds(len_ref, q_pos)[0]
        tops = []
        for cols in chunks:
            s = jnp.where(sq == sk[0:1, cols], dot(q, kvt[:, cols]), -jnp.inf)
            s_ref[:, cols] = s
            tops.append(jnp.max(s, axis=1, keepdims=True))
        shift = functools.reduce(jnp.maximum, tops) * exp_scale
        sums = []
        for cols in chunks:
            e = jnp.exp2(s_ref[:, cols] * exp_scale - shift)
            s_ref[:, cols] = e
            sums.append(jnp.sum(e, axis=1, keepdims=True))
        inv = 1.0 / functools.reduce(jnp.add, sums)
        o = jnp.zeros((q_rows, LANES), F32)
        g_t = qgt[HD:LANES, i * q_rows:(i + 1) * q_rows]
        for cols in chunks:
            probs = s_ref[:, cols] * inv
            s_ref[:, cols] = probs
            low_probs = probs.astype(BF16)
            o = o + dot(low_probs, keys_of(cols))
            acc[HD:LANES, cols] += dot(g_t, low_probs)
        rowdot = jnp.sum(g.astype(F32) * o, axis=1, keepdims=True)
        dq = jnp.zeros((q_rows, LANES), F32)
        q_t = qgt[0:HD, i * q_rows:(i + 1) * q_rows]
        for cols in chunks:
            dscores = (s_ref[:, cols] * (dot(g, kvt[:, cols]) - rowdot)).astype(BF16)
            dq = dq + dot(dscores, keys_of(cols))
            acc[0:HD, cols] += dot(q_t, dscores)
        ad[own] = jnp.where(q_low, dq * scale, o).astype(BF16).reshape(QB, rows, LANES)
        for r in range(QB):
            ad_start(i * QB + r)

    def turn_back(i, carry):
        cols = lane_block(i)
        both = jnp.concatenate([acc[0:HD, cols] * scale, acc[HD:LANES, cols]], axis=0)
        kvt2[side, :, cols] = both.astype(BF16)
        kv[i] = jnp.transpose(both).astype(BF16)
        kv_start(i)
        return carry

    def swap(source, target, send, recv, peer):
        return pltpu.make_async_remote_copy(
            source, target, send, recv, device_id={"ctx": peer}, device_id_type=MESH
        )

    steps = n // QB
    early = first_key(steps - 1)
    spans = [slice(0, early), slice(early, total)]

    def across_part(k, who):
        part = kvt2.at[who, :, spans[k]]
        return swap(part, part, across_send.at[k], across_recv.at[k], across)

    mate_copy = swap(hall.at[core], hall.at[core], mate_send, mate_recv, mate)
    mate_arrival = swap(hall.at[1 - core], hall.at[1 - core], mate_send, mate_recv, mate)

    for i in range(steps):
        attend(i)
        final = total if i == steps - 1 else first_key(i + 1)
        lax.fori_loop(first_key(i) // rows, final // rows, turn_back, 0)
        if i == steps - 2:
            across_part(0, side).start()
            h_wait()
            mate_copy.start()
    across_part(1, side).start()
    rad[me] = ad[me]
    rkv[me] = kv[me]

    ad_wait()

    def attended_block(p, carry):
        cols = lane_block(p)
        even, odd = rad[2 * p].astype(F32), rad[2 * p + 1].astype(F32)
        dquery = jnp.where(low, even, roll_half(odd))
        attended = jnp.where(low, roll_half(even), odd)
        out_ref[0, :, cols] = (hb[:, cols].astype(F32) + attended).astype(BF16)
        dh[p] = cot[:, cols].astype(F32) + dquery
        return carry

    lax.fori_loop(0, blocks, attended_block, 0, unroll=2)
    kv_wait()

    def grad_block(p, carry):
        even, odd = rkv[2 * p].astype(F32), rkv[2 * p + 1].astype(F32)
        kvg[:, lane_block(p)] = jnp.where(low, even, roll_half(odd)).astype(BF16)
        kvg[:, lane_block(p + blocks)] = jnp.where(low, roll_half(even), odd).astype(BF16)
        return carry

    lax.fori_loop(0, blocks, grad_block, 0, unroll=4)

    def dhidden_block(b, carry):
        back = dot_last(kvg[...], wkv[lane_block(b, 256), :])
        for half in range(2):
            p = 2 * b + half
            dhidden = dh[p] + back[:, half * LANES:(half + 1) * LANES]
            dh[p] = dhidden
            v = conv[p]
            s = 1.0 / (1.0 + jnp.exp(-v))
            dcb[:, lane_block(p)] = (dhidden * (s * (1.0 + v * (1.0 - s)))).astype(BF16)
        return carry

    lax.fori_loop(0, blocks // 2, dhidden_block, 0, unroll=2)

    halos2 = halo_copies(dcb, halo2, halo2_send, halo2_recv)
    for copy in halos2:
        copy.start()

    def tap_grads_block(b, carry):
        cols = lane_block(b)
        own = dcb[:, cols].astype(F32)
        pad[b, RIM:RIM + rows] = own
        for j in range(TAPS):
            a, r = divmod(j, 8)
            source = masked(taps_in(j, slice(0, rows)), xs[r, b, 8 * a:8 * a + rows])
            pdw[j:j + 1, cols] = jnp.sum(source * own, axis=0, keepdims=True)
        turned = jnp.transpose(pdw[:, cols])
        for half in range(2):
            packed = None
            for k in range(4):
                slab = turned[half * HD + 16 * k:half * HD + 16 * (k + 1)]
                slab = slab if k == 0 else pltpu.roll(slab, 32 * k, 1)
                packed = slab if packed is None else packed + slab
            w1s[2 * b + half] = packed
        return carry

    lax.fori_loop(0, blocks, tap_grads_block, 0)

    def w1_to(s):
        other = lax.rem(seq + s, m)
        return pltpu.make_async_remote_copy(
            w1s.at[other], w1r.at[seq], w1_send.at[other], w1_recv.at[seq],
            device_id={"dp": other}, device_id_type=MESH,
        )

    def w1_start(s, carry):
        w1_to(s).start()
        return carry

    lax.fori_loop(1, m, w1_start, 0)
    w1r[seq] = w1s[seq]

    mate_arrival.wait_recv()
    for k in range(2):
        across_part(k, 1 - side).wait_recv()
    for k in range(2):
        part = jnp.transpose(dot(kvt2[...].reshape(2 * LANES, total), hall[k].reshape(total, width // 4)))
        for q in range(m // 4):
            for e in range(2):
                piece = part[q * HD:(q + 1) * HD, e * LANES:(e + 1) * LANES]
                g1s[2 * (k * (m // 4) + q) + e] = piece.astype(BF16)

    def g1_copy(index):
        q, e = lax.div(index, 2), lax.rem(index, 2)
        return pltpu.make_async_remote_copy(
            g1s.at[index], g1r.at[seq], g1_send.at[index], g1_recv.at[seq],
            device_id={"dp": 2 * q + side, "ctx": 4 * ring_spot + 2 * e + core}, device_id_type=MESH,
        )

    stays = lax.rem(seq, 2) == side
    own_piece = 2 * lax.div(seq, 2) + side

    def g1_start(index, carry):
        @pl.when(jnp.logical_not(stays & (index == own_piece)))
        def _():
            g1_copy(index).start()
        return carry

    lax.fori_loop(0, m, g1_start, 0)

    @pl.when(stays)
    def _():
        g1r[seq] = g1s[own_piece]

    for copy in halos2:
        copy.wait()

    def dframes_block(b, carry):
        cols = lane_block(b)
        pad[b, 0:RIM] = halo2[0, :, cols].astype(F32)
        pad[b, RIM + rows:2 * RIM + rows] = halo2[1, :, cols].astype(F32)
        for r in range(8):
            ys[r] = pad[b, r + 1:r + 1 + rows + 24]
        result = dh[b]
        for j in range(TAPS):
            a, r = divmod(j, 8)
            back = TAPS - 1 - j
            source = masked(taps_in(j, slice(0, rows)), ys[r, 8 * a:8 * a + rows])
            result = result + source * wdw[back:back + 1, cols]
        dfr_ref[0, :, cols] = result.astype(BF16)
        return carry

    lax.fori_loop(0, LATE, dframes_block, 0)

    def g1_wait(d, carry):
        @pl.when(jnp.logical_not((d == seq) & stays))
        def _():
            pltpu.make_async_remote_copy(
                g1s.at[0], g1r.at[d], g1_send.at[0], g1_recv.at[d],
                device_id={"ctx": mate}, device_id_type=MESH,
            ).wait_recv()
        return carry

    def w1_wait(s, carry):
        d = lax.rem(seq + s, m)
        pltpu.make_async_remote_copy(
            w1s.at[d], w1r.at[d], w1_send.at[d], w1_recv.at[d],
            device_id={"dp": d}, device_id_type=MESH,
        ).wait_recv()
        return carry

    lax.fori_loop(1, m, w1_wait, 0)
    lax.fori_loop(0, m, g1_wait, 0)
    kv_rows = functools.reduce(jnp.add, [g1r[d].astype(F32) for d in range(m)])
    dw_rows = functools.reduce(jnp.add, [w1r[d] for d in range(m)])
    for k in range(4):
        turned = dw_rows if k == 0 else pltpu.roll(dw_rows, LANES - 32 * k, 1)
        for r in range(4):
            c = 4 * k + r
            s2[c, 0:4] = kv_rows[4 * c:4 * c + 4]
            s2[c, 4:8] = turned[4 * r:4 * r + 4]
    t2_start()
    t2[me] = s2[me]

    lax.fori_loop(LATE, blocks, dframes_block, 0)

    g_sent()
    q_sent()
    f_sent()
    h_sent()
    ad_sent()
    kv_sent()
    mate_copy.wait_send()
    for k in range(2):
        across_part(k, side).wait_send()

    def g1_sent(index, carry):
        @pl.when(jnp.logical_not(stays & (index == own_piece)))
        def _():
            g1_copy(index).wait_send()
        return carry

    lax.fori_loop(0, m, g1_sent, 0)

    def w1_sent(s, carry):
        w1_to(s).wait_send()
        return carry

    lax.fori_loop(1, m, w1_sent, 0)
    t2_wait()
    low4 = lax.broadcasted_iota(I32, (4, LANES), 1) < HD
    for p in range(blocks):
        even, odd = t2[2 * p, 0:4], t2[2 * p + 1, 0:4]
        gkv_ref[:, p * LANES:(p + 1) * LANES] = jnp.where(low4, even, roll_half(odd))
        gkv_ref[:, width + p * LANES:width + (p + 1) * LANES] = jnp.where(low4, roll_half(even), odd)
    gdw_ref[...] = functools.reduce(jnp.add, [t2[h, 4:8] for h in range(n)])[:, 0:TAPS]
    t2_sent()


def hand_out(*refs):
    sources, targets, stages, sems = refs[:4], refs[4:8], refs[8:12], refs[12]
    loads = [pltpu.make_async_copy(a, b, sems.at[0, k]) for k, (a, b) in enumerate(zip(sources, stages))]
    stores = [pltpu.make_async_copy(a, b, sems.at[1, k]) for k, (a, b) in enumerate(zip(stages, targets))]
    for load in loads:
        load.start()
    for load, store in zip(loads, stores):
        load.wait()
        store.start()
    for store in stores:
        store.wait()


def on_device(frames, utt_lengths, cotangent, w_dw, w_kv):
    n = lax.axis_size("ctx")
    rows, width = frames.shape[1], frames.shape[2]
    blocks = width // LANES
    total = n * rows
    dma = pltpu.SemaphoreType.DMA
    vmem = pltpu.VMEM
    scratch = [
        vmem((rows, width), BF16),
        vmem((rows, width), BF16),
        vmem(w_dw.shape, F32),
        vmem(w_kv.shape, BF16),
        vmem((2, RIM, width), BF16),
        vmem((2, RIM, width), BF16),
        vmem((blocks, rows + 2 * RIM, LANES), F32),
        vmem((8, blocks, rows + 24, LANES), F32),
        vmem((8, rows + 24, LANES), F32),
        vmem((rows, LANES), I32),
        vmem((rows, LANES), I32),
        vmem((blocks, rows, LANES), F32),
        vmem((rows, width), BF16),
        vmem((n, rows // 2, LANES), BF16),
        vmem((n, rows // 2, LANES), BF16),
        vmem((n, rows // 2, LANES), BF16),
        vmem((n, rows // 2, LANES), BF16),
        vmem((n, rows, LANES), BF16),
        vmem((n, rows, LANES), BF16),
        vmem((4, rows, width // 4), BF16),
        vmem((2, n, rows, width // 4), BF16),
        vmem((n, rows, LANES), BF16),
        vmem((LANES, total), BF16),
        vmem((LANES, total), BF16),
        vmem((8, total), I32),
        vmem((QB * rows, total), F32),
        vmem((LANES, total), F32),
        vmem((n, rows, LANES), BF16),
        vmem((n, rows, LANES), BF16),
        vmem((n, rows, LANES), BF16),
        vmem((n, rows, LANES), BF16),
        vmem((2, LANES, total), BF16),
        vmem((rows, 2 * width), BF16),
        vmem((blocks, rows, LANES), F32),
        vmem((rows, width), BF16),
        vmem((n, HD, LANES), BF16),
        vmem((n, HD, LANES), BF16),
        vmem((LANES, width), F32),
        vmem((n, 16, LANES), F32),
        vmem((n, 16, LANES), F32),
        vmem((n, 8, LANES), F32),
        vmem((n, 8, LANES), F32),
        dma((4,)), dma((2,)), dma((2,)), dma((2,)), dma((2,)),
        dma((n,)), dma((n,)), dma((n,)), dma((n,)), dma((n,)), dma((n,)), dma((n,)), dma((n,)),
        dma((n,)), dma((n,)), dma((n,)), dma((n,)), dma, dma, dma((2,)), dma((2,)), dma((n,)), dma((n,)),
        dma((n,)), dma((n,)), dma((n,)), dma((n,)),
    ]
    whole = pl.BlockSpec(memory_space=vmem)
    anywhere = pl.BlockSpec(memory_space=pl.ANY)
    in_hbm = pl.BlockSpec(memory_space=pltpu.HBM)
    results = (
        jax.ShapeDtypeStruct(frames.shape, BF16),
        jax.ShapeDtypeStruct(frames.shape, BF16),
        jax.ShapeDtypeStruct((4, 2 * width), F32),
        jax.ShapeDtypeStruct((4, TAPS), F32),
    )
    raw = pl.pallas_call(
        functools.partial(kernel, n),
        out_shape=results,
        in_specs=[pl.BlockSpec(memory_space=pltpu.SMEM), anywhere, anywhere, anywhere, anywhere],
        out_specs=(whole,) * 4,
        scratch_shapes=scratch,
        compiler_params=pltpu.CompilerParams(
            collective_id=0, has_side_effects=True, vmem_limit_bytes=56 << 20
        ),
    )(utt_lengths, frames, cotangent, w_dw, w_kv)
    return pl.pallas_call(
        hand_out, out_shape=results, in_specs=[in_hbm] * 4, out_specs=(in_hbm,) * 4,
        scratch_shapes=[vmem(r.shape, r.dtype) for r in results] + [dma((2, 4))],
    )(*raw)


def solution(mesh):
    placed = (P("dp", "ctx", None), P("dp", None), P("dp", "ctx", None), P(), P())
    return jax.shard_map(
        on_device,
        mesh=mesh,
        in_specs=placed,
        out_specs=(
            P("dp", "ctx", None),
            P("dp", "ctx", None),
            P(("dp", "ctx"), None),
            P(("dp", "ctx"), None),
        ),
        check_vma=False,
    )
```

```python
import functools
import math

import jax
import jax.numpy as jnp
from jax import lax
from jax.experimental import pallas as pl
from jax.experimental.pallas import tpu as pltpu
from jax.sharding import PartitionSpec as P

F32, BF16, I32 = jnp.float32, jnp.bfloat16, jnp.int32
MESH = pl.DeviceIdType.MESH
HD = 64
LANES = 128
TAPS = 31
RIM = 16
FAR = 1 << 20
QB = 2
MOST = 1152
LATE = 6


def dot(a, b):
    return jnp.dot(a, b, preferred_element_type=F32)


def dot_last(a, b):
    return lax.dot_general(a, b, (((1,), (1,)), ((), ())), preferred_element_type=F32)


def lane_block(index, width=LANES):
    return pl.ds(pl.multiple_of(index * width, width), width)


def utt_bounds(len_ref, pos):
    end = jnp.int32(0)
    start_of = jnp.zeros(pos.shape, I32)
    end_of = jnp.full(pos.shape, FAR, I32)
    for u in range(len_ref.shape[1]):
        end = end + len_ref[0, u]
        start_of = jnp.where(end <= pos, end, start_of)
        end_of = jnp.minimum(end_of, jnp.where(end > pos, end, FAR))
    return start_of, end_of


def kernel(
    n,
    len_ref, fr_hbm, cot_hbm, wdw_hbm, wkv_hbm,
    out_ref, dfr_ref, gkv_ref, gdw_ref,
    fr, cot, wdw, wkv, halo, halo2, pad, xs, ys, jlo, jhi, conv, hb,
    g_snd, g_rcv, q_snd, q_rcv, f_snd, f_rcv, hp, hall,
    qg, qgt, kvt, sk, s_ref, acc, ad, kv, rad, rkv, kvt2,
    kvg, dh, dcb, g1s, g1r, pdw, w1s, w1r, s2, t2,
    local_sems, halo_send, halo_recv, halo2_send, halo2_recv,
    g_send, g_recv, q_send, q_recv, f_send, f_recv, h_send, h_recv,
    ad_send, ad_recv, kv_send, kv_recv, mate_send, mate_recv, across_send, across_recv, g1_send, g1_recv,
    w1_send, w1_recv, t2_send, t2_recv,
):
    rows, width = fr.shape
    blocks = width // LANES
    total = n * rows
    m = n
    me = lax.axis_index("ctx")
    seq = lax.axis_index("dp")
    core = lax.rem(me, 2)
    chip = lax.div(me, 2)
    mate = me + 1 - 2 * core
    side = lax.rem(chip, 2)
    across = me + 2 - 4 * side
    ring_spot = lax.div(chip, 2)
    scale = 1.0 / math.sqrt(HD)

    barrier = pltpu.get_barrier_semaphore()

    def greet_ctx(s, carry):
        pl.semaphore_signal(barrier, inc=1, device_id={"ctx": lax.rem(me + s, n)}, device_id_type=MESH)
        return carry

    def greet_dp(s, carry):
        other = lax.rem(seq + s, m)
        pl.semaphore_signal(barrier, inc=1, device_id={"dp": other}, device_id_type=MESH)
        pl.semaphore_signal(barrier, inc=1, device_id={"dp": other, "ctx": across}, device_id_type=MESH)
        return carry

    fr_copy = pltpu.make_async_copy(fr_hbm.at[0], fr, local_sems.at[0])
    wdw_copy = pltpu.make_async_copy(wdw_hbm, wdw, local_sems.at[1])
    cot_copy = pltpu.make_async_copy(cot_hbm.at[0], cot, local_sems.at[2])
    wkv_copy = pltpu.make_async_copy(wkv_hbm, wkv, local_sems.at[3])
    lax.fori_loop(1, m, greet_dp, 0)
    lax.fori_loop(1, n, greet_ctx, 0)
    for copy in (fr_copy, wdw_copy, cot_copy, wkv_copy):
        copy.start()

    low = lax.broadcasted_iota(I32, (rows, LANES), 1) < HD
    low_half = lax.broadcasted_iota(I32, (rows // 2, LANES), 1) < HD
    pos = me * rows + lax.broadcasted_iota(I32, (rows, LANES), 0)
    start_of, end_of = utt_bounds(len_ref, pos)
    jlo[...] = start_of - pos + TAPS // 2
    jhi[...] = end_of - pos + TAPS // 2

    def taps_in(j, part):
        if j < TAPS // 2:
            return j >= jlo[part]
        if j > TAPS // 2:
            return j < jhi[part]
        return None

    def masked(mask, value):
        return value if mask is None else jnp.where(mask, value, 0.0)

    def conv_part(b, first, last):
        cols = lane_block(b)
        part = slice(first, last)
        result = jnp.zeros((last - first, LANES), F32)
        for j in range(TAPS):
            a, r = divmod(j, 8)
            source = xs[r, b, 8 * a + first:8 * a + last]
            result = result + masked(taps_in(j, part), source) * wdw[j:j + 1, cols]
        conv[b, part] = result
        hidden = pad[b, RIM + first:RIM + last] + result / (1.0 + jnp.exp(-result))
        hb[part, cols] = hidden.astype(BF16)

    def conv_inner(b, carry):
        pad[b, RIM:RIM + rows] = fr[:, lane_block(b)].astype(F32)
        for r in range(8):
            xs[r, b, RIM:rows + 8] = pad[b, r + 1 + RIM:r + 1 + rows + 8]
        conv_part(b, RIM, rows - RIM)
        return carry

    def roll_half(x):
        return pltpu.roll(x, HD, 1)

    def split_heads(pair, target, p):
        top, bottom = pair[0:rows // 2], pair[rows // 2:]
        target[2 * p] = jnp.where(low_half, top, roll_half(bottom)).astype(BF16)
        target[2 * p + 1] = jnp.where(low_half, roll_half(top), bottom).astype(BF16)

    def pack_cotangent(p, carry):
        split_heads(cot[:, lane_block(p)].astype(F32), g_snd, p)
        return carry

    cot_copy.wait()
    lax.fori_loop(0, blocks, pack_cotangent, 0)
    fr_copy.wait()

    pl.semaphore_wait(barrier, (n - 1) + 2 * (m - 1))

    right, left = lax.rem(me + 1, n), lax.rem(me + n - 1, n)

    def halo_copies(source, target, send, recv):
        return (
            pltpu.make_async_remote_copy(
                source.at[pl.ds(rows - RIM, RIM)], target.at[0], send.at[0], recv.at[0],
                device_id={"ctx": right}, device_id_type=MESH,
            ),
            pltpu.make_async_remote_copy(
                source.at[pl.ds(0, RIM)], target.at[1], send.at[1], recv.at[1],
                device_id={"ctx": left}, device_id_type=MESH,
            ),
        )

    def exchange(source_of, target, send, recv):
        def copy_to(peer):
            return pltpu.make_async_remote_copy(
                source_of(peer), target(peer).at[me], send.at[peer], recv.at[me],
                device_id={"ctx": peer}, device_id_type=MESH,
            )

        def copy_from(peer):
            return pltpu.make_async_remote_copy(
                source_of(peer), target(me).at[peer], send.at[peer], recv.at[peer],
                device_id={"ctx": peer}, device_id_type=MESH,
            )

        def start(s, carry):
            copy_to(lax.rem(me + s, n)).start()
            return carry

        def start_one(peer):
            @pl.when(peer != me)
            def _():
                copy_to(peer).start()

        def wait_recv(s, carry):
            copy_from(lax.rem(me + n - s, n)).wait_recv()
            return carry

        def wait_send(s, carry):
            copy_to(lax.rem(me + s, n)).wait_send()
            return carry

        return (
            lambda first=1, last=n: lax.fori_loop(first, last, start, 0),
            start_one,
            lambda: lax.fori_loop(1, n, wait_recv, 0),
            lambda: lax.fori_loop(1, n, wait_send, 0),
        )

    g_start, _, g_wait, g_sent = exchange(lambda peer: g_snd.at[peer], lambda owner: g_rcv, g_send, g_recv)
    q_start, _, q_wait, q_sent = exchange(lambda peer: q_snd.at[peer], lambda owner: q_rcv, q_send, q_recv)
    _, f_start, f_wait, f_sent = exchange(lambda peer: f_snd.at[peer], lambda owner: f_rcv, f_send, f_recv)
    h_start, _, h_wait, h_sent = exchange(lambda peer: hp.at[lax.rem(peer, 4)], lambda owner: hall.at[lax.rem(owner, 2)], h_send, h_recv)
    _, ad_start, ad_wait, ad_sent = exchange(lambda peer: ad.at[peer], lambda owner: rad, ad_send, ad_recv)
    _, kv_start, kv_wait, kv_sent = exchange(lambda peer: kv.at[peer], lambda owner: rkv, kv_send, kv_recv)
    t2_start, _, t2_wait, t2_sent = exchange(lambda peer: s2.at[peer], lambda owner: t2, t2_send, t2_recv)

    halos = halo_copies(fr, halo, halo_send, halo_recv)
    for copy in halos:
        copy.start()
    g_start()
    wdw_copy.wait()
    pad[:, 0:RIM] = jnp.zeros((blocks, RIM, LANES), F32)
    pad[:, RIM + rows:2 * RIM + rows] = jnp.zeros((blocks, RIM, LANES), F32)
    lax.fori_loop(0, blocks, conv_inner, 0)
    sk[...] = utt_bounds(len_ref, lax.broadcasted_iota(I32, (8, total), 1))[0]
    acc[...] = jnp.zeros(acc.shape, F32)
    pdw[...] = jnp.zeros(pdw.shape, F32)
    for copy in halos:
        copy.wait()

    def conv_outer(b, carry):
        cols = lane_block(b)
        pad[b, 0:RIM] = halo[0, :, cols].astype(F32)
        pad[b, RIM + rows:2 * RIM + rows] = halo[1, :, cols].astype(F32)
        for r in range(8):
            xs[r, b, 0:RIM] = pad[b, r + 1:r + 1 + RIM]
            xs[r, b, rows + 8:rows + 24] = pad[b, r + 9 + rows:r + 25 + rows]
        conv_part(b, 0, RIM)
        conv_part(b, rows - RIM, rows)
        return carry

    lax.fori_loop(0, blocks, conv_outer, 0, unroll=4)

    def pack_hidden(b, carry):
        first, second = [hb[:, lane_block(2 * b + k)].astype(F32) for k in range(2)]
        split_heads(first, q_snd, 2 * b)
        split_heads(second, q_snd, 2 * b + 1)
        return carry

    def pack_gather(b, carry):
        first, second = [hb[:, lane_block(2 * b + k)].astype(F32) for k in range(2)]
        part = lane_block(lax.rem(b, 2))
        hp[lax.div(b, 2), :, part] = jnp.where(low, first, roll_half(second)).astype(BF16)
        hp[2 + lax.div(b, 2), :, part] = jnp.where(low, roll_half(first), second).astype(BF16)
        return carry

    lax.fori_loop(0, blocks // 2, pack_hidden, 0, unroll=2)
    q_start()
    wkv_copy.wait()

    def kv_block(b, carry):
        k_cols = dot(hb[...], wkv[:, lane_block(b, 256)])
        v_cols = dot(hb[...], wkv[:, lane_block(b + blocks // 2, 256)])
        for half in range(2):
            h = 2 * (2 * b + half)
            k2 = k_cols[:, half * LANES:(half + 1) * LANES]
            v2 = v_cols[:, half * LANES:(half + 1) * LANES]
            f_snd[h] = jnp.where(low, k2, roll_half(v2)).astype(BF16)
            f_snd[h + 1] = jnp.where(low, roll_half(k2), v2).astype(BF16)
            f_start(h)
            f_start(h + 1)
        return carry

    lax.fori_loop(0, blocks // 2, kv_block, 0, unroll=2)
    lax.fori_loop(0, blocks // 2, pack_gather, 0)
    g_rcv[me] = g_snd[me]
    q_rcv[me] = q_snd[me]
    f_rcv[me] = f_snd[me]
    hall[core, me] = hp[2 * side + core]
    g_wait()
    q_wait()

    def turn_queries(i, carry):
        q2, g2 = q_rcv[i].astype(F32), g_rcv[i].astype(F32)
        both = jnp.concatenate(
            [jnp.where(low_half, q2, roll_half(g2)), jnp.where(low_half, roll_half(q2), g2)], axis=0
        )
        qg[i] = both.astype(BF16)
        qgt[:, lane_block(i)] = jnp.transpose(both).astype(BF16)
        return carry

    lax.fori_loop(0, n, turn_queries, 0, unroll=4)
    f_wait()
    h_start()

    def turn_keys(i, carry):
        kvt[:, lane_block(i)] = jnp.transpose(f_rcv[i].astype(F32)).astype(BF16)
        return carry

    lax.fori_loop(0, n, turn_keys, 0, unroll=4)

    q_rows = QB * rows
    q_low = lax.broadcasted_iota(I32, (q_rows, LANES), 1) < HD
    exp_scale = scale * math.log2(math.e)

    def first_key(i):
        return min(max(0, i * q_rows - (MOST - 1)) // rows * rows, total)

    def last_key(i):
        return min(total, -(-((i + 1) * q_rows - 1 + MOST) // rows) * rows)

    def attend(i):
        own = slice(i * QB, (i + 1) * QB)
        chunks = [slice(first_key(i), last_key(i))]

        def keys_of(cols):
            return f_rcv[cols.start // rows:cols.stop // rows].reshape(cols.stop - cols.start, LANES)

        both = qg[own].reshape(q_rows, LANES)
        zero = jnp.zeros_like(both)
        q, g = jnp.where(q_low, both, zero), jnp.where(q_low, zero, both)
        q_pos = i * q_rows + lax.broadcasted_iota(I32, (q_rows, 1), 0)
        sq = utt_bounds(len_ref, q_pos)[0]
        tops = []
        for cols in chunks:
            s = jnp.where(sq == sk[0:1, cols], dot(q, kvt[:, cols]), -jnp.inf)
            s_ref[:, cols] = s
            tops.append(jnp.max(s, axis=1, keepdims=True))
        shift = functools.reduce(jnp.maximum, tops) * exp_scale
        sums = []
        for cols in chunks:
            e = jnp.exp2(s_ref[:, cols] * exp_scale - shift)
            s_ref[:, cols] = e
            sums.append(jnp.sum(e, axis=1, keepdims=True))
        inv = 1.0 / functools.reduce(jnp.add, sums)
        o = jnp.zeros((q_rows, LANES), F32)
        g_t = qgt[HD:LANES, i * q_rows:(i + 1) * q_rows]
        for cols in chunks:
            probs = s_ref[:, cols] * inv
            s_ref[:, cols] = probs
            low_probs = probs.astype(BF16)
            o = o + dot(low_probs, keys_of(cols))
            acc[HD:LANES, cols] += dot(g_t, low_probs)
        rowdot = jnp.sum(g.astype(F32) * o, axis=1, keepdims=True)
        dq = jnp.zeros((q_rows, LANES), F32)
        q_t = qgt[0:HD, i * q_rows:(i + 1) * q_rows]
        for cols in chunks:
            dscores = (s_ref[:, cols] * (dot(g, kvt[:, cols]) - rowdot)).astype(BF16)
            dq = dq + dot(dscores, keys_of(cols))
            acc[0:HD, cols] += dot(q_t, dscores)
        ad[own] = jnp.where(q_low, dq * scale, o).astype(BF16).reshape(QB, rows, LANES)
        for r in range(QB):
            ad_start(i * QB + r)

    def turn_back(i, carry):
        cols = lane_block(i)
        both = jnp.concatenate([acc[0:HD, cols] * scale, acc[HD:LANES, cols]], axis=0)
        kvt2[side, :, cols] = both.astype(BF16)
        kv[i] = jnp.transpose(both).astype(BF16)
        kv_start(i)
        return carry

    def swap(source, target, send, recv, peer):
        return pltpu.make_async_remote_copy(
            source, target, send, recv, device_id={"ctx": peer}, device_id_type=MESH
        )

    steps = n // QB
    early = first_key(steps - 1)
    spans = [slice(0, early), slice(early, total)]

    def across_part(k, who):
        part = kvt2.at[who, :, spans[k]]
        return swap(part, part, across_send.at[k], across_recv.at[k], across)

    mate_copy = swap(hall.at[core], hall.at[core], mate_send, mate_recv, mate)
    mate_arrival = swap(hall.at[1 - core], hall.at[1 - core], mate_send, mate_recv, mate)

    for i in range(steps):
        attend(i)
        final = total if i == steps - 1 else first_key(i + 1)
        lax.fori_loop(first_key(i) // rows, final // rows, turn_back, 0)
        if i == steps - 2:
            across_part(0, side).start()
            h_wait()
            mate_copy.start()
    across_part(1, side).start()
    rad[me] = ad[me]
    rkv[me] = kv[me]

    ad_wait()

    def attended_block(p, carry):
        cols = lane_block(p)
        even, odd = rad[2 * p].astype(F32), rad[2 * p + 1].astype(F32)
        dquery = jnp.where(low, even, roll_half(odd))
        attended = jnp.where(low, roll_half(even), odd)
        out_ref[0, :, cols] = (hb[:, cols].astype(F32) + attended).astype(BF16)
        dh[p] = cot[:, cols].astype(F32) + dquery
        return carry

    lax.fori_loop(0, blocks, attended_block, 0, unroll=2)
    kv_wait()

    def grad_block(p, carry):
        even, odd = rkv[2 * p].astype(F32), rkv[2 * p + 1].astype(F32)
        kvg[:, lane_block(p)] = jnp.where(low, even, roll_half(odd)).astype(BF16)
        kvg[:, lane_block(p + blocks)] = jnp.where(low, roll_half(even), odd).astype(BF16)
        return carry

    lax.fori_loop(0, blocks, grad_block, 0, unroll=4)

    def dhidden_block(b, carry):
        back = dot_last(kvg[...], wkv[lane_block(b, 256), :])
        for half in range(2):
            p = 2 * b + half
            dhidden = dh[p] + back[:, half * LANES:(half + 1) * LANES]
            dh[p] = dhidden
            v = conv[p]
            s = 1.0 / (1.0 + jnp.exp(-v))
            dcb[:, lane_block(p)] = (dhidden * (s * (1.0 + v * (1.0 - s)))).astype(BF16)
        return carry

    lax.fori_loop(0, blocks // 2, dhidden_block, 0, unroll=2)

    halos2 = halo_copies(dcb, halo2, halo2_send, halo2_recv)
    for copy in halos2:
        copy.start()

    def tap_grads_block(b, carry):
        cols = lane_block(b)
        own = dcb[:, cols].astype(F32)
        pad[b, RIM:RIM + rows] = own
        for j in range(TAPS):
            a, r = divmod(j, 8)
            source = masked(taps_in(j, slice(0, rows)), xs[r, b, 8 * a:8 * a + rows])
            pdw[j:j + 1, cols] = jnp.sum(source * own, axis=0, keepdims=True)
        turned = jnp.transpose(pdw[:, cols])
        for half in range(2):
            packed = None
            for k in range(4):
                slab = turned[half * HD + 16 * k:half * HD + 16 * (k + 1)]
                slab = slab if k == 0 else pltpu.roll(slab, 32 * k, 1)
                packed = slab if packed is None else packed + slab
            w1s[2 * b + half] = packed
        return carry

    lax.fori_loop(0, blocks, tap_grads_block, 0)

    def w1_to(s):
        other = lax.rem(seq + s, m)
        return pltpu.make_async_remote_copy(
            w1s.at[other], w1r.at[seq], w1_send.at[other], w1_recv.at[seq],
            device_id={"dp": other}, device_id_type=MESH,
        )

    def w1_start(s, carry):
        w1_to(s).start()
        return carry

    lax.fori_loop(1, m, w1_start, 0)
    w1r[seq] = w1s[seq]

    mate_arrival.wait_recv()
    for k in range(2):
        across_part(k, 1 - side).wait_recv()
    for k in range(2):
        part = jnp.transpose(dot(kvt2[...].reshape(2 * LANES, total), hall[k].reshape(total, width // 4)))
        for q in range(m // 4):
            for e in range(2):
                piece = part[q * HD:(q + 1) * HD, e * LANES:(e + 1) * LANES]
                g1s[2 * (k * (m // 4) + q) + e] = piece.astype(BF16)

    def g1_copy(index):
        q, e = lax.div(index, 2), lax.rem(index, 2)
        return pltpu.make_async_remote_copy(
            g1s.at[index], g1r.at[seq], g1_send.at[index], g1_recv.at[seq],
            device_id={"dp": 2 * q + side, "ctx": 4 * ring_spot + 2 * e + core}, device_id_type=MESH,
        )

    stays = lax.rem(seq, 2) == side
    own_piece = 2 * lax.div(seq, 2) + side

    def g1_start(index, carry):
        @pl.when(jnp.logical_not(stays & (index == own_piece)))
        def _():
            g1_copy(index).start()
        return carry

    lax.fori_loop(0, m, g1_start, 0)

    @pl.when(stays)
    def _():
        g1r[seq] = g1s[own_piece]

    for copy in halos2:
        copy.wait()

    def dframes_block(b, carry):
        cols = lane_block(b)
        pad[b, 0:RIM] = halo2[0, :, cols].astype(F32)
        pad[b, RIM + rows:2 * RIM + rows] = halo2[1, :, cols].astype(F32)
        for r in range(8):
            ys[r] = pad[b, r + 1:r + 1 + rows + 24]
        result = dh[b]
        for j in range(TAPS):
            a, r = divmod(j, 8)
            back = TAPS - 1 - j
            source = masked(taps_in(j, slice(0, rows)), ys[r, 8 * a:8 * a + rows])
            result = result + source * wdw[back:back + 1, cols]
        dfr_ref[0, :, cols] = result.astype(BF16)
        return carry

    lax.fori_loop(0, LATE, dframes_block, 0)

    def g1_wait(d, carry):
        @pl.when(jnp.logical_not((d == seq) & stays))
        def _():
            pltpu.make_async_remote_copy(
                g1s.at[0], g1r.at[d], g1_send.at[0], g1_recv.at[d],
                device_id={"ctx": mate}, device_id_type=MESH,
            ).wait_recv()
        return carry

    def w1_wait(s, carry):
        d = lax.rem(seq + s, m)
        pltpu.make_async_remote_copy(
            w1s.at[d], w1r.at[d], w1_send.at[d], w1_recv.at[d],
            device_id={"dp": d}, device_id_type=MESH,
        ).wait_recv()
        return carry

    lax.fori_loop(1, m, w1_wait, 0)
    lax.fori_loop(0, m, g1_wait, 0)
    kv_rows = functools.reduce(jnp.add, [g1r[d].astype(F32) for d in range(m)])
    dw_rows = functools.reduce(jnp.add, [w1r[d] for d in range(m)])
    for k in range(4):
        turned = dw_rows if k == 0 else pltpu.roll(dw_rows, LANES - 32 * k, 1)
        for r in range(4):
            c = 4 * k + r
            s2[c, 0:4] = kv_rows[4 * c:4 * c + 4]
            s2[c, 4:8] = turned[4 * r:4 * r + 4]
    t2_start()
    t2[me] = s2[me]

    lax.fori_loop(LATE, blocks, dframes_block, 0)

    g_sent()
    q_sent()
    f_sent()
    h_sent()
    ad_sent()
    kv_sent()
    mate_copy.wait_send()
    for k in range(2):
        across_part(k, side).wait_send()

    def g1_sent(index, carry):
        @pl.when(jnp.logical_not(stays & (index == own_piece)))
        def _():
            g1_copy(index).wait_send()
        return carry

    lax.fori_loop(0, m, g1_sent, 0)

    def w1_sent(s, carry):
        w1_to(s).wait_send()
        return carry

    lax.fori_loop(1, m, w1_sent, 0)
    t2_wait()
    low4 = lax.broadcasted_iota(I32, (4, LANES), 1) < HD
    for p in range(blocks):
        even, odd = t2[2 * p, 0:4], t2[2 * p + 1, 0:4]
        gkv_ref[:, p * LANES:(p + 1) * LANES] = jnp.where(low4, even, roll_half(odd))
        gkv_ref[:, width + p * LANES:width + (p + 1) * LANES] = jnp.where(low4, roll_half(even), odd)
    gdw_ref[...] = functools.reduce(jnp.add, [t2[h, 4:8] for h in range(n)])[:, 0:TAPS]
    t2_sent()


def hand_out(*refs):
    sources, targets, stages, sems = refs[:4], refs[4:8], refs[8:12], refs[12]
    loads = [pltpu.make_async_copy(a, b, sems.at[0, k]) for k, (a, b) in enumerate(zip(sources, stages))]
    stores = [pltpu.make_async_copy(a, b, sems.at[1, k]) for k, (a, b) in enumerate(zip(stages, targets))]
    for load in loads:
        load.start()
    for load, store in zip(loads, stores):
        load.wait()
        store.start()
    for store in stores:
        store.wait()


def on_device(frames, utt_lengths, cotangent, w_dw, w_kv):
    n = lax.axis_size("ctx")
    rows, width = frames.shape[1], frames.shape[2]
    blocks = width // LANES
    total = n * rows
    dma = pltpu.SemaphoreType.DMA
    vmem = pltpu.VMEM
    scratch = [
        vmem((rows, width), BF16),
        vmem((rows, width), BF16),
        vmem(w_dw.shape, F32),
        vmem(w_kv.shape, BF16),
        vmem((2, RIM, width), BF16),
        vmem((2, RIM, width), BF16),
        vmem((blocks, rows + 2 * RIM, LANES), F32),
        vmem((8, blocks, rows + 24, LANES), F32),
        vmem((8, rows + 24, LANES), F32),
        vmem((rows, LANES), I32),
        vmem((rows, LANES), I32),
        vmem((blocks, rows, LANES), F32),
        vmem((rows, width), BF16),
        vmem((n, rows // 2, LANES), BF16),
        vmem((n, rows // 2, LANES), BF16),
        vmem((n, rows // 2, LANES), BF16),
        vmem((n, rows // 2, LANES), BF16),
        vmem((n, rows, LANES), BF16),
        vmem((n, rows, LANES), BF16),
        vmem((4, rows, width // 4), BF16),
        vmem((2, n, rows, width // 4), BF16),
        vmem((n, rows, LANES), BF16),
        vmem((LANES, total), BF16),
        vmem((LANES, total), BF16),
        vmem((8, total), I32),
        vmem((QB * rows, total), F32),
        vmem((LANES, total), F32),
        vmem((n, rows, LANES), BF16),
        vmem((n, rows, LANES), BF16),
        vmem((n, rows, LANES), BF16),
        vmem((n, rows, LANES), BF16),
        vmem((2, LANES, total), BF16),
        vmem((rows, 2 * width), BF16),
        vmem((blocks, rows, LANES), F32),
        vmem((rows, width), BF16),
        vmem((n, HD, LANES), BF16),
        vmem((n, HD, LANES), BF16),
        vmem((LANES, width), F32),
        vmem((n, 16, LANES), F32),
        vmem((n, 16, LANES), F32),
        vmem((n, 8, LANES), F32),
        vmem((n, 8, LANES), F32),
        dma((4,)), dma((2,)), dma((2,)), dma((2,)), dma((2,)),
        dma((n,)), dma((n,)), dma((n,)), dma((n,)), dma((n,)), dma((n,)), dma((n,)), dma((n,)),
        dma((n,)), dma((n,)), dma((n,)), dma((n,)), dma, dma, dma((2,)), dma((2,)), dma((n,)), dma((n,)),
        dma((n,)), dma((n,)), dma((n,)), dma((n,)),
    ]
    whole = pl.BlockSpec(memory_space=vmem)
    anywhere = pl.BlockSpec(memory_space=pl.ANY)
    in_hbm = pl.BlockSpec(memory_space=pltpu.HBM)
    results = (
        jax.ShapeDtypeStruct(frames.shape, BF16),
        jax.ShapeDtypeStruct(frames.shape, BF16),
        jax.ShapeDtypeStruct((4, 2 * width), F32),
        jax.ShapeDtypeStruct((4, TAPS), F32),
    )
    raw = pl.pallas_call(
        functools.partial(kernel, n),
        out_shape=results,
        in_specs=[pl.BlockSpec(memory_space=pltpu.SMEM), anywhere, anywhere, anywhere, anywhere],
        out_specs=(whole,) * 4,
        scratch_shapes=scratch,
        compiler_params=pltpu.CompilerParams(
            collective_id=0, has_side_effects=True, vmem_limit_bytes=56 << 20
        ),
    )(utt_lengths, frames, cotangent, w_dw, w_kv)
    return pl.pallas_call(
        hand_out, out_shape=results, in_specs=[in_hbm] * 4, out_specs=(in_hbm,) * 4,
        scratch_shapes=[vmem(r.shape, r.dtype) for r in results] + [dma((2, 4))],
    )(*raw)


def solution(mesh):
    placed = (P("dp", "ctx", None), P("dp", None), P("dp", "ctx", None), P(), P())
    return jax.shard_map(
        on_device,
        mesh=mesh,
        in_specs=placed,
        out_specs=(
            P("dp", "ctx", None),
            P("dp", "ctx", None),
            P(("dp", "ctx"), None),
            P(("dp", "ctx"), None),
        ),
        check_vma=False,
    )
```
